256 devices in a mesh: slab: 64 (over z, y, core), thick: 4 (over x).
Axes of the slice: x: 4, y: 4, z: 8, core: 2. Of those that a mesh axis runs over, the one named last changes fastest.
Arguments:
- ref_pos: float32 [3, 4194304], P(None, ('slab', 'thick')), may hold values from 0 to 8
- displacement: float32 [3, 4194304], P(None, ('slab', 'thick')), may hold values from -1 to 1
- weighted_volume: float32 [4194304], P(('slab', 'thick')), may hold values from 10 to 100
- ghost_corner_lists: int32 [2, 2, 4096], P(None, None, ('slab', 'thick')), may hold values from 0 to 127
- bond_row_tiles: int32 [32768], P(('slab', 'thick')), may hold values from 0 to 127
- bond_column_tiles: int32 [32768], P(('slab', 'thick')), may hold values from 0 to 319, as said below
- bond_count: int32 [256], P(('slab', 'thick')), may hold values from 32 to 128, as said below
- bond_masks: int32 [32768, 16, 128], P(('slab', 'thick')), may hold values from 0 to 255
- broken_bonds: int32 [32768, 16, 128], P(('slab', 'thick')), may hold values from 0 to 255
Outputs:
- force: float32 [3, 4194304], P(None, ('slab', 'thick'))
- dilatation: float32 [4194304], P(('slab', 'thick'))
The draws below stay inside these ranges and needn't reach their ends.
Inputs may be any that keep to these rules, and one draw needn't show every extreme that they name: `bond_column_tiles`: an entry c below 128 names an owned tile; an entry at or above it names cycle cell (c - 128) // 16, only of neighbours that exist. `bond_count`: some device has exactly 128 live slots in every draw; live slots come first.
All inputs are finite; a program needn't handle non-finite values.
Results may differ from the reference program's by a relative error of at most 0.00015.
Values sent between devices are 32-bit elements; how exact they have to be, the bound alone decides.
No kernel may reach another device: no remote copies, remote signals or barrier semaphores. Data moves between devices by JAX's collectives and lax.ppermute only.
A program may use at most 64 MiB of HBM per device.

```python
import math
import jax
import jax.numpy as jnp
from jax import lax

TILES_DEV = 128
GHOST = 16
BOND_TILES = 128
POINTS = 4194304
SLOTS = 32768
LISTS = 4096
N_SLAB = 64
N_THICK = 4
DEVICES = 256


def draw_bond_column_tiles(key, part):
    total = DEVICES * BOND_TILES
    keys = jax.random.split(key, 4)
    device_ids = jnp.arange(total, dtype=jnp.int32) // BOND_TILES
    slab_pos = device_ids // N_THICK
    thick_pos = device_ids % N_THICK
    cycle_table = jnp.array([0, 1, 2, 3, 4, 7, 8, 11, 12, 13, 14, 15], dtype=jnp.int32)
    cycle_cell = jax.random.randint(keys[0], (total,), 0, 12)
    position = cycle_table[cycle_cell]
    row_cell = position // 4
    col_cell = position % 4
    slab_step = jnp.where(row_cell == 0, -1, jnp.where(row_cell == 3, 1, 0))
    thick_step = jnp.where(col_cell == 0, -1, jnp.where(col_cell == 3, 1, 0))
    exists = (slab_pos + slab_step >= 0) & (slab_pos + slab_step < N_SLAB) & (thick_pos + thick_step >= 0) & (thick_pos + thick_step < N_THICK)
    choose_ghost = jax.random.randint(keys[1], (total,), 0, 2) == 1
    member = jax.random.randint(keys[2], (total,), 0, GHOST)
    owned = jax.random.randint(keys[3], (total,), 0, TILES_DEV)
    return jnp.where(exists & choose_ghost, TILES_DEV + cycle_cell * GHOST + member, owned).astype(jnp.int32)


def draw_bond_count(key, part):
    keys = jax.random.split(key, 2)
    counts = jax.random.randint(keys[0], (DEVICES,), BOND_TILES // 4, BOND_TILES + 1)
    busiest = jax.random.randint(keys[1], (), 0, DEVICES)
    return jnp.where(jnp.arange(DEVICES) == busiest, BOND_TILES, counts).astype(jnp.int32)


def with_ends(drawn, own_key, least, high):
    longest = drawn.shape.index(max(drawn.shape))
    spots = []
    for shift in (0, 1):
        where = [jax.random.randint(jax.random.fold_in(own_key, axis), (), 0, length) for axis, length in enumerate(drawn.shape)]
        where[longest] = (where[longest] + shift) % drawn.shape[longest]
        spots.append(tuple(where))
    return drawn.at[spots[0]].set(least).at[spots[1]].set(high)


def level_of(rng, dims, shards, least, largest):
    level = 1.0
    for dim, blocks in shards:
        heights = jax.random.uniform(jax.random.fold_in(jax.random.fold_in(rng, 6), dim), (blocks,), jnp.float32, least / len(shards), largest / len(shards))
        level = level * jnp.repeat(jnp.exp(heights), dims[dim] // blocks).reshape((-1,) + (1,) * (len(dims) - 1 - dim))
    return level


def normal_values(key, dims, scale, bound, cuts=(), held_as=jnp.bfloat16):
    drawn = jax.random.normal(key, dims, jnp.float32) * scale
    if len(cuts) > 0:
        drawn = level_of(key, dims, cuts, -0.22, 0.18) * drawn
    return jnp.clip(drawn, min=-bound, max=bound).astype(held_as)


def setup_inputs(seed: int = 0) -> dict:
    arg_keys = jax.random.split(jax.random.key(seed), 10)
    return {
        "ref_pos": jnp.clip(8.0 * jax.random.uniform(arg_keys[0], (3, POINTS), jnp.float32) ** level_of(arg_keys[0], (3, POINTS), ((1, 256),), -0.2, 0.2), 0.0, 8.0),
        "displacement": normal_values(arg_keys[1], (3, POINTS), 0.2, 1.0, ((1, 256),), jnp.float32),
        "weighted_volume": jnp.clip(jnp.exp(math.log(100.0) - 2.3025851 * jax.random.uniform(arg_keys[2], (POINTS,), jnp.float32) ** level_of(arg_keys[2], (POINTS,), ((0, 256),), -0.2, 0.2)), 10.0, 100.0),
        "ghost_corner_lists": with_ends(jax.random.randint(arg_keys[3], (2, 2, LISTS), 0, TILES_DEV), jax.random.fold_in(arg_keys[3], 1), 0, TILES_DEV - 1).astype(jnp.int32),
        "bond_row_tiles": with_ends(jax.random.randint(arg_keys[4], (SLOTS,), 0, TILES_DEV), jax.random.fold_in(arg_keys[4], 1), 0, TILES_DEV - 1).astype(jnp.int32),
        "bond_column_tiles": draw_bond_column_tiles(jax.random.fold_in(arg_keys[9], 71), 0),
        "bond_count": draw_bond_count(jax.random.fold_in(arg_keys[9], 71), 0),
        "bond_masks": with_ends(jax.random.randint(arg_keys[7], (SLOTS, 16, 128), 0, 256), jax.random.fold_in(arg_keys[7], 1), 0, 255).astype(jnp.int32),
        "broken_bonds": with_ends(jax.random.randint(arg_keys[8], (SLOTS, 16, 128), 0, 256), jax.random.fold_in(arg_keys[8], 1), 0, 255).astype(jnp.int32),
    }


young = 25.0
poisson = 0.22
bulk_modulus = young / (3.0 * (1.0 - 2.0 * poisson))
shear_modulus = young / (2.0 * (1.0 + poisson))
volumetric_term = 3.0 * bulk_modulus - 5.0 * shear_modulus
shear_term = 15.0 * shear_modulus
radius_floor = 0.5
cycle_cells = (0, 1, 2, 3, 4, 7, 8, 11, 12, 13, 14, 15)

def unpack_words(packed):
    shifts = jnp.arange(8, dtype=jnp.int32)
    spread = jnp.right_shift(packed[:, :, None, :], shifts[None, None, :, None]) & 1
    return spread.reshape(packed.shape[0], 128, 128).astype(jnp.float32)

def bond_geometry(row_payload, column_payload, packed_mask_words, fractured_bit_words, own_tile_list, active_slot_flags):
    ref_vec = column_payload[0:3, :, None, :] - row_payload[0:3, :, :, None]
    cur_vec = ref_vec + (column_payload[3:6, :, None, :] - row_payload[3:6, :, :, None])
    ref_len = jnp.maximum(jnp.sqrt(lax.optimization_barrier(jnp.sum(ref_vec * ref_vec, axis=0))), radius_floor)
    cur_len = jnp.maximum(jnp.sqrt(lax.optimization_barrier(jnp.sum(cur_vec * cur_vec, axis=0))), radius_floor)
    stretch = cur_len - ref_len
    below_diag = jnp.arange(128)[:, None] < jnp.arange(128)[None, :]
    keep_pair = jnp.where(own_tile_list[:, None, None], below_diag[None], True) & active_slot_flags[:, None, None]
    unbroken_flags = unpack_words(packed_mask_words) * (1.0 - unpack_words(fractured_bit_words)) * keep_pair.astype(jnp.float32)
    return (unbroken_flags, ref_len, cur_len, stretch, cur_vec)

def stretch_terms(row_payload, column_payload, packed_mask_words, fractured_bit_words, own_tile_list, active_slot_flags):
    unbroken_flags, ref_len, cur_len, stretch, cur_vec = bond_geometry(row_payload, column_payload, packed_mask_words, fractured_bit_words, own_tile_list, active_slot_flags)
    weighted = unbroken_flags * stretch
    return (lax.optimization_barrier(jnp.sum(weighted, axis=2)), lax.optimization_barrier(jnp.sum(weighted, axis=1)))

def force_contributions(row_payload, column_payload, packed_mask_words, fractured_bit_words, own_tile_list, active_slot_flags, row_dilatation, column_dilatation):
    unbroken_flags, ref_len, cur_len, stretch, cur_vec = bond_geometry(row_payload, column_payload, packed_mask_words, fractured_bit_words, own_tile_list, active_slot_flags)
    per_unit_length = shear_term * stretch / ref_len
    gathered_row = unbroken_flags * (volumetric_term * row_dilatation[:, :, None] + per_unit_length) / row_payload[6][:, :, None]
    gathered_column = unbroken_flags * (volumetric_term * column_dilatation[:, None, :] + per_unit_length) / column_payload[6][:, None, :]
    weight = (gathered_row + gathered_column) / cur_len
    pair_force = weight[None] * cur_vec
    return (lax.optimization_barrier(jnp.sum(pair_force, axis=3)), -lax.optimization_barrier(jnp.sum(pair_force, axis=2)))

def reference(ref_pos, displacement, weighted_volume, ghost_corner_lists, bond_row_tiles, bond_column_tiles, bond_count, bond_masks, broken_bonds):
    total_tiles = DEVICES * TILES_DEV
    point_state = jnp.concatenate([ref_pos, displacement, weighted_volume[None]], 0).reshape(7, total_tiles, 128)
    box_lists = ghost_corner_lists.reshape(2, 2, DEVICES, GHOST)
    device_ids = jnp.arange(DEVICES, dtype=jnp.int32)
    slab_pos = device_ids // N_THICK
    thick_pos = device_ids % N_THICK
    ghost_ids = []
    for cycle_cell in cycle_cells:
        row_cell = cycle_cell // 4
        col_cell = cycle_cell % 4
        slab_step = -1 if row_cell == 0 else 1 if row_cell == 3 else 0
        thick_step = -1 if col_cell == 0 else 1 if col_cell == 3 else 0
        slab_side = 1 if row_cell == 0 else 0 if row_cell == 3 else row_cell - 1
        thick_side = 1 if col_cell == 0 else 0 if col_cell == 3 else col_cell - 1
        near_slab = jnp.clip(slab_pos + slab_step, 0, N_SLAB - 1)
        near_thick = jnp.clip(thick_pos + thick_step, 0, N_THICK - 1)
        neighbour = (near_slab * N_THICK + near_thick).astype(jnp.int32)
        ghost_ids.append(neighbour[:, None] * TILES_DEV + box_lists[slab_side, thick_side][neighbour])
    ghost_table = jnp.stack(ghost_ids, 1).reshape(DEVICES, 12 * GHOST).astype(jnp.int32)
    rows_dev = bond_row_tiles.reshape(DEVICES, BOND_TILES)
    cols_dev = bond_column_tiles.reshape(DEVICES, BOND_TILES)
    ghost_slot = jnp.clip(cols_dev - TILES_DEV, 0, 12 * GHOST - 1).astype(jnp.int32)
    ghost_ref = jnp.take_along_axis(ghost_table, ghost_slot, axis=1)
    row_ids = (device_ids[:, None] * TILES_DEV + rows_dev).reshape(-1).astype(jnp.int32)
    col_ids = jnp.where(cols_dev < TILES_DEV, device_ids[:, None] * TILES_DEV + cols_dev, ghost_ref).reshape(-1).astype(jnp.int32)
    own_tile_list = (cols_dev == rows_dev).reshape(-1)
    active_slot_flags = (jnp.arange(BOND_TILES)[None, :] < bond_count[:, None]).reshape(-1)
    ref_width = 64
    block_total = DEVICES * BOND_TILES // ref_width

    def pieces(block_index):
        offset = block_index * ref_width
        ids_row = lax.dynamic_slice_in_dim(row_ids, offset, ref_width)
        ids_col = lax.dynamic_slice_in_dim(col_ids, offset, ref_width)
        return (ids_row, ids_col, jnp.take(point_state, ids_row, axis=1), jnp.take(point_state, ids_col, axis=1), lax.dynamic_slice_in_dim(bond_masks, offset, ref_width, 0), lax.dynamic_slice_in_dim(broken_bonds, offset, ref_width, 0), lax.dynamic_slice_in_dim(own_tile_list, offset, ref_width), lax.dynamic_slice_in_dim(active_slot_flags, offset, ref_width))

    def first_pass(block_index):
        ids_row, ids_col, row_payload, column_payload, masks_blk, broken_blk, self_blk, live_blk = pieces(block_index)
        return stretch_terms(row_payload, column_payload, masks_blk, broken_blk, self_blk, live_blk)
    row_terms, col_terms = lax.map(first_pass, jnp.arange(block_total, dtype=jnp.int32))
    stretch_sum = jax.ops.segment_sum(row_terms.reshape(-1, 128), row_ids, total_tiles) + jax.ops.segment_sum(col_terms.reshape(-1, 128), col_ids, total_tiles)
    dilatation = 3.0 * stretch_sum / point_state[6]

    def second_pass(block_index):
        ids_row, ids_col, row_payload, column_payload, masks_blk, broken_blk, self_blk, live_blk = pieces(block_index)
        return force_contributions(row_payload, column_payload, masks_blk, broken_blk, self_blk, live_blk, jnp.take(dilatation, ids_row, axis=0), jnp.take(dilatation, ids_col, axis=0))
    row_force, col_force = lax.map(second_pass, jnp.arange(block_total, dtype=jnp.int32))
    row_force = jnp.moveaxis(row_force, 1, 2).reshape(-1, 3, 128)
    col_force = jnp.moveaxis(col_force, 1, 2).reshape(-1, 3, 128)
    force_sum = jax.ops.segment_sum(row_force, row_ids, total_tiles) + jax.ops.segment_sum(col_force, col_ids, total_tiles)
    force = jnp.moveaxis(force_sum, 1, 0).reshape(3, total_tiles * 128)
    return (force, dilatation.reshape(total_tiles * 128))
```

```python
import functools

import jax
import jax.numpy as jnp
from jax import lax
from jax.experimental import pallas as pl
from jax.experimental.pallas import tpu as pltpu
from jax.sharding import PartitionSpec as P

young = 25.0
poisson = 0.22
bulk_modulus = young / (3.0 * (1.0 - 2.0 * poisson))
shear_modulus = young / (2.0 * (1.0 + poisson))
volumetric_term = 3.0 * bulk_modulus - 5.0 * shear_modulus
shear_term = 15.0 * shear_modulus
radius_floor = 0.5
floor_squared = radius_floor * radius_floor

TILES = 128
SLOTS = 128
GHOST = 16
CELLS = 12
LISTS = 4 * GHOST
GHOST_AT = 136
COUNT_AT = 272
META = 280

f32 = jnp.float32
bf16 = jnp.bfloat16
KROWS = 48
i32 = jnp.int32
VM = pl.BlockSpec(memory_space=pltpu.VMEM)
SM = pl.BlockSpec(memory_space=pltpu.SMEM)


def shape(*dims, dtype=f32):
    return jax.ShapeDtypeStruct(dims, dtype)


def call(kernel, name, outs, ins, out_spaces=None, aliases=None, scratch=(), flops=0):
    def run(*args):
        return pl.pallas_call(
            kernel,
            out_shape=outs,
            in_specs=list(ins),
            out_specs=list(out_spaces or [VM] * len(outs)),
            scratch_shapes=list(scratch),
            input_output_aliases=aliases or {},
            compiler_params=pltpu.CompilerParams(vmem_limit_bytes=24 << 20),
            cost_estimate=pl.CostEstimate(flops=flops, bytes_accessed=1 << 20, transcendentals=0),
            name=name,
        )(*args)

    return run


def bcast_row(row):
    return jnp.broadcast_to(row, (8, 128))


def lane(column):
    return jnp.broadcast_to(column, (8, 128))


def fold(block):
    return jnp.sum(block, axis=0, keepdims=True)


def decode(code):
    return code & 255, (code >> 8) & 255, code >> 16


def over_slots(meta, base, count, half, body, unroll=2):
    total = lax.div(count + (unroll - 1), unroll)
    mid = lax.div(total + 1, 2)
    lo, hi = {None: (0, total), 0: (0, mid), 1: (mid, total)}[half]

    def step(i, carry):
        for u in range(unroll):
            body(*decode(meta[base + i * unroll + u]))
        return carry

    lax.fori_loop(lo, hi, step, 0)


def bit_mask(bits, k, w, probe):
    return (bcast_row(bits[k, w : w + 1, :]) & probe) != 0


def probe_bits():
    return jnp.left_shift(jnp.int32(1), lax.broadcasted_iota(i32, (8, 128), 0))


def pack_kernel(x, u, m, lists, rows, cols, count, table, low, high, meta, psi):
    psi[...] = shear_term / m[...]
    zero = jnp.zeros((1, 128), f32)

    def tile(t, carry):
        at = pl.ds(pl.multiple_of(t * 128, 128), 128)
        table[t, 0:3, :] = x[:, at]
        table[t, 3:6, :] = u[:, at]
        table[t, 6:7, :] = psi[pl.ds(t, 1), :]
        table[t, 7:8, :] = zero
        return carry

    lax.fori_loop(0, TILES, tile, 0, unroll=8)
    for side, out in ((0, low), (1, high)):
        for g in range(2 * GHOST):
            out[g] = table[lists[side * 2 * GHOST + g]]

    def sort(k, carry):
        nl, ng = carry
        b = cols[k]
        code = k + rows[k] * 256 + b * 65536
        ghost = (b >= TILES).astype(i32)
        meta[nl] = code
        meta[GHOST_AT + ng] = code
        return nl + 1 - ghost, ng + ghost

    nl, ng = lax.fori_loop(0, count[0], sort, (jnp.int32(0), jnp.int32(0)))
    meta[nl] = SLOTS
    meta[GHOST_AT + ng] = SLOTS + TILES * 65536
    meta[COUNT_AT] = nl
    meta[COUNT_AT + 1] = ng


def columns_of(tab, b, names):
    return [bcast_row(tab[b, c : c + 1, :]) for c in names]


def split3(v):
    hi = v.astype(bf16).astype(f32)
    rest = v - hi
    mid = rest.astype(bf16).astype(f32)
    return hi, mid, rest - mid


def selector(names):
    wide = 128 * len(names)
    k = lax.broadcasted_iota(i32, (KROWS, wide), 0) & 15
    n = lax.broadcasted_iota(i32, (KROWS, wide), 1) >> 7
    want = jnp.zeros((KROWS, wide), i32) - 1
    for at, c in enumerate(names):
        want = jnp.where(n == at, c, want)
    return jnp.where(k == want, 1.0, 0.0).astype(bf16)


def spread(tall, a, sel):
    return jnp.dot(tall[a], sel[...], preferred_element_type=f32)


def spread_phi(tall_phi, sel_phi, a):
    return jnp.dot(tall_phi[a >> 4], sel_phi[a & 15], preferred_element_type=f32)


def piece(rows, w, c):
    return rows[8 * w : 8 * w + 8, 128 * c : 128 * c + 128]


def bond(rows, cols, w):
    xi = [cols[c] - piece(rows, w, c) for c in range(3)]
    y = [xi[c] + (cols[3 + c] - piece(rows, w, 3 + c)) for c in range(3)]
    r2 = jnp.maximum(xi[0] * xi[0] + xi[1] * xi[1] + xi[2] * xi[2], floor_squared)
    s2 = jnp.maximum(y[0] * y[0] + y[1] * y[1] + y[2] * y[2], floor_squared)
    rinv = lax.rsqrt(r2)
    sinv = lax.rsqrt(s2)
    e = s2 * sinv - r2 * rinv
    return y, e, rinv, sinv


def unit(rows, cols, w):
    y = [cols[c] - piece(rows, w, c) for c in range(3)]
    s2 = jnp.maximum(y[0] * y[0] + y[1] * y[1] + y[2] * y[2], floor_squared)
    return y, lax.rsqrt(s2)


def lane_sum(block):
    return jnp.sum(block, axis=1, keepdims=True)


def merge3(parts):
    lan = lax.broadcasted_iota(i32, (8, 128), 1)
    return jnp.where(lan == 0, lane(parts[0]), jnp.where(lan == 1, lane(parts[1]), lane(parts[2])))


def stretch_slot(tall, sel, other, base, bits, probe, row_acc, col_acc):
    def body(k, a, b):
        bb = b - base
        row = spread(tall, a, sel)
        cols = columns_of(other, bb, range(6))
        down = None
        across = []
        for w in range(16):
            y, e, rinv, sinv = bond(row, cols, w)
            e = jnp.where(bit_mask(bits, k, w, probe), e, 0.0)
            down = e if down is None else down + e
            across.append(lane(lane_sum(e)))
        sums = jnp.transpose(jnp.concatenate(across, 0))[0:1, :]
        row_acc[pl.ds(a, 1), :] += sums
        col_acc[pl.ds(bb, 1), :] += fold(down)

    return body


def local_stretch_kernel(half, meta, tab, *refs):
    if half == 0:
        masks, broken, bits, acc, tall, sel_phi, sel = refs
        acc[...] = jnp.zeros_like(acc)

        def stand(t, carry):
            moved = jnp.concatenate([tab[t, 0:3, :] + tab[t, 3:6, :], jnp.zeros((5, 128), f32)], 0)
            parts = split3(jnp.concatenate([tab[t], moved], 0))
            tall[t] = jnp.transpose(jnp.concatenate(parts, 0)).astype(bf16)
            return carry

        lax.fori_loop(0, TILES, stand, 0, unroll=2)
        k = lax.broadcasted_iota(i32, (128, 128), 0)
        for n in range(16):
            sel_phi[n] = jnp.where(((k >> 3) == n) & ((k & 7) < 3), 1.0, 0.0).astype(bf16)

        def clear(k, carry):
            bits[k] = masks[k] & ~broken[k]
            return carry

        lax.fori_loop(0, SLOTS, clear, 0, unroll=4)
        bits[SLOTS] = jnp.zeros((16, 128), i32)
        w = lax.broadcasted_iota(i32, (16, 128), 0)
        j = lax.broadcasted_iota(i32, (16, 128), 1)
        below = jnp.zeros((16, 128), i32)
        for b in range(8):
            below += jnp.where(8 * w + b < j, 1 << b, 0)

        def own(i, carry):
            k, a, b = decode(meta[i])

            @pl.when(a == b)
            def _():
                bits[k] = bits[k] & below

            return carry

        lax.fori_loop(0, meta[COUNT_AT], own, 0)
    else:
        bits, tall, unused, acc, sel = refs
    sel[...] = selector(range(6))
    probe = probe_bits()
    over_slots(
        meta,
        0,
        meta[COUNT_AT],
        half,
        stretch_slot(tall, sel, tab, 0, bits, probe, acc, acc),
    )


def row_of(cell):
    return cell // 4, cell % 4


cycle_cells = (0, 1, 2, 3, 4, 7, 8, 11, 12, 13, 14, 15)


def ghost_stretch_kernel(
    meta, tall, bits, low, high, left, right, unused, acc, ghosts, to_left, to_right, middle, gacc,
    sel,
):
    for n, cell in enumerate(cycle_cells):
        r, c = row_of(cell)
        if c == 0:
            src, at = left, r * GHOST
        elif c == 3:
            src, at = right, r * GHOST
        else:
            src, at = (low if r == 0 else high), (c - 1) * GHOST
        ghosts[n * GHOST : (n + 1) * GHOST] = src[at : at + GHOST]
    gacc[...] = jnp.zeros_like(gacc)
    sel[...] = selector(range(6))
    probe = probe_bits()
    over_slots(
        meta,
        GHOST_AT,
        meta[COUNT_AT + 1],
        None,
        stretch_slot(tall, sel, ghosts, TILES, bits, probe, acc, gacc),
    )
    for n, cell in enumerate(cycle_cells):
        r, c = row_of(cell)
        part = gacc[n * GHOST : (n + 1) * GHOST, :]
        if c == 0:
            to_left[r] = part
        elif c == 3:
            to_right[r] = part
        else:
            middle[2 * (r // 3) + c - 1] = part


def ghost_terms_kernel(half, meta, tall, ghosts, bits, *refs):
    if half == 0:
        rows_out, cols_out, sel = refs
        rows_out[...] = jnp.zeros_like(rows_out)
        cols_out[...] = jnp.zeros_like(cols_out)
    else:
        unused0, unused1, rows_out, cols_out, sel = refs
    sel[...] = selector(range(7))
    probe = probe_bits()

    def body(k, a, b):
        bb = b - TILES
        row = spread(tall, a, sel)
        cols = columns_of(ghosts, bb, range(7))
        down = [None] * 6
        across = []
        for w in range(16):
            y, e, rinv, sinv = bond(row, cols, w)
            g = (e * rinv) * (cols[6] + piece(row, w, 6))
            keep = jnp.where(bit_mask(bits, k, w, probe), sinv, 0.0)
            v = [keep * y[c] for c in range(3)]
            p = [g * v[c] for c in range(3)]
            down = [q if d is None else d + q for d, q in zip(down, p + v)]
            across.append(merge3([lane_sum(q) for q in p]))
        sums = jnp.transpose(jnp.concatenate(across, 0))
        rows_out[a, 0:3, :] += sums[0:3, :]
        for c in range(6):
            cols_out[bb, c : c + 1, :] += fold(down[c])

    over_slots(meta, GHOST_AT, meta[COUNT_AT + 1], half, body)


def dilatation_kernel(
    meta, lists, tab_in, tall, sel_phi, ghosts, bits, acc_in, m, from_left, from_right, from_low,
    from_high, terms_in, terms, tab, tall_phi, dil, to_left, to_right, middle, acc, parts, sel,
):
    acc[...] = acc_in[...]
    thick = (from_left, from_right)
    for s in range(2):
        slab = (from_low, from_high)[s]
        for t in range(2):
            for g in range(GHOST):
                q = lists[(2 * s + t) * GHOST + g]
                acc[pl.ds(q, 1), :] += thick[t][1 + s, g : g + 1, :] + slab[t, g : g + 1, :]
    theta = 3.0 * acc[...] / m[...]
    dil[...] = theta
    acc[...] = volumetric_term * theta / m[...]

    parts[...] = jnp.zeros_like(parts)

    def tile(t, carry):
        phi = acc[pl.ds(t, 1), :]
        tab[t, 7:8, :] = phi
        for n, part in enumerate(split3(phi)):
            parts[t, n : n + 1, :] = part
        return carry

    lax.fori_loop(0, TILES, tile, 0, unroll=8)
    for n in range(8):
        block = parts[16 * n : 16 * n + 16].reshape(128, 128)
        tall_phi[n] = jnp.transpose(block).astype(bf16)
    sel[...] = selector(range(8, 11))
    probe = probe_bits()

    def body(k, a, b):
        bb = b - TILES
        row = spread(tall, a, sel)
        phi_row = spread_phi(tall_phi, sel_phi, a)
        cols = [bcast_row(ghosts[bb, c : c + 1, :] + ghosts[bb, 3 + c : 4 + c, :]) for c in range(3)]
        down = [None] * 3
        for w in range(16):
            y, sinv = unit(row, cols, w)
            keep = jnp.where(bit_mask(bits, k, w, probe), sinv * piece(phi_row, w, 0), 0.0)
            v = [keep * y[c] for c in range(3)]
            down = [q if d is None else d + q for d, q in zip(down, v)]
        for c in range(3):
            terms[bb, c : c + 1, :] += fold(down[c])

    over_slots(meta, GHOST_AT, meta[COUNT_AT + 1], None, body)
    for n, cell in enumerate(cycle_cells):
        r, c = row_of(cell)
        if c == 0:
            out, at = to_left, r * GHOST
        elif c == 3:
            out, at = to_right, r * GHOST
        else:
            out, at = middle, (2 * (r // 3) + c - 1) * GHOST
        out[at : at + GHOST] = terms[n * GHOST : (n + 1) * GHOST]
    for t, out in ((0, to_left), (1, to_right)):
        for s in range(2):
            for g in range(GHOST):
                phi = acc[pl.ds(lists[(2 * s + t) * GHOST + g], 1), :]
                out[s * GHOST + g, 6:7, :] = phi
                middle[(2 * s + t) * GHOST + g, 6:7, :] = phi


def relay_kernel(from_left, from_right, middle, to_low, to_high):
    thick = (from_left, from_right)
    for s, out in ((0, to_low), (1, to_high)):
        for t in range(2):
            for g in range(GHOST):
                n, at = t * GHOST + g, (2 * s + t) * GHOST + g
                far = thick[t][3 * s * GHOST + g]
                out[n, 0:6, :] = middle[at, 0:6, :] + far[0:6, :]
                out[n, 6:7, :] = middle[at, 6:7, :]
                out[n, 7:8, :] = thick[t][s * GHOST + g, 6:7, :]


def local_force_kernel(half, meta, tab, tall, tall_phi, sel_phi, bits, *refs):
    if half == 0:
        acc, sel = refs
        acc[...] = jnp.zeros_like(acc)
    else:
        unused, acc, sel = refs
    sel[...] = selector(range(7))
    probe = probe_bits()

    def body(k, a, b):
        row = spread(tall, a, sel)
        phi_row = spread_phi(tall_phi, sel_phi, a)
        cols = columns_of(tab, b, range(8))
        down = [None] * 3
        across = []
        for w in range(16):
            y, e, rinv, sinv = bond(row, cols, w)
            g = (e * rinv) * (cols[6] + piece(row, w, 6)) + (cols[7] + piece(phi_row, w, 0))
            keep = jnp.where(bit_mask(bits, k, w, probe), sinv * g, 0.0)
            v = [keep * y[c] for c in range(3)]
            down = [q if d is None else d + q for d, q in zip(down, v)]
            across.append(merge3([lane_sum(q) for q in v]))
        sums = jnp.transpose(jnp.concatenate(across, 0))
        acc[a, 0:3, :] += sums[0:3, :]
        for c in range(3):
            acc[b, c : c + 1, :] -= fold(down[c])

    over_slots(meta, 0, meta[COUNT_AT], half, body)


def force_kernel(
    meta, lists, tab, tall, tall_phi, sel_phi, ghosts, bits, local, rows_in, from_left, from_right,
    from_low, from_high, force, acc, sel, gphi,
):
    for n, cell in enumerate(cycle_cells):
        r, c = row_of(cell)
        if r in (0, 3):
            src, at, line = (from_low if r == 0 else from_high), (c // 2) * GHOST, (7, 6, 6, 7)[c]
        else:
            src, at, line = (from_left if c == 0 else from_right), (r - 1) * GHOST, 6
        for g in range(GHOST):
            gphi[n * GHOST + g : n * GHOST + g + 1, :] = src[at + g, line : line + 1, :]

    def tile(t, carry):
        acc[t] = local[t] + rows_in[t]
        return carry

    lax.fori_loop(0, TILES, tile, 0, unroll=8)
    sel[...] = selector(range(8, 11))
    probe = probe_bits()

    def body(k, a, b):
        bb = b - TILES
        row = spread(tall, a, sel)
        phi_row = spread_phi(tall_phi, sel_phi, a)
        cols = [bcast_row(ghosts[bb, c : c + 1, :] + ghosts[bb, 3 + c : 4 + c, :]) for c in range(3)]
        phi = bcast_row(gphi[pl.ds(bb, 1), :])
        across = []
        for w in range(16):
            y, sinv = unit(row, cols, w)
            both = phi + piece(phi_row, w, 0)
            keep = jnp.where(bit_mask(bits, k, w, probe), sinv * both, 0.0)
            across.append(merge3([lane_sum(keep * y[c]) for c in range(3)]))
        sums = jnp.transpose(jnp.concatenate(across, 0))
        acc[a, 0:3, :] += sums[0:3, :]

    over_slots(meta, GHOST_AT, meta[COUNT_AT + 1], None, body)
    thick = (from_left, from_right)
    for s in range(2):
        slab = (from_low, from_high)[s]
        for t in range(2):
            for g in range(GHOST):
                q = lists[(2 * s + t) * GHOST + g]
                for src, at in ((thick[t], (1 + s) * GHOST + g), (slab, t * GHOST + g)):
                    acc[q, 0:3, :] -= src[at, 0:3, :] + tab[q, 7:8, :] * src[at, 3:6, :]

    def store(t, carry):
        force[:, pl.ds(pl.multiple_of(t * 128, 128), 128)] = acc[t, 0:3, :]
        return carry

    lax.fori_loop(0, TILES, store, 0, unroll=8)


def shifts(axis):
    count = lax.axis_size(axis)
    forward = [(i, i + 1) for i in range(count - 1)]
    return forward, [(target, source) for source, target in forward]


def swap(to_low, to_high, axis):
    forward, backward = shifts(axis)
    return lax.ppermute(to_high, axis, forward), lax.ppermute(to_low, axis, backward)


def body(
    ref_pos, displacement, weighted_volume, corner_lists, row_tiles, column_tiles, bond_count,
    masks, broken,
):
    m = weighted_volume.reshape(TILES, 128)
    lists = corner_lists.reshape(LISTS)
    table, low, high, meta = call(
        pack_kernel,
        "pack",
        (
            shape(TILES, 8, 128),
            shape(2 * GHOST, 8, 128),
            shape(2 * GHOST, 8, 128),
            shape(META, dtype=i32),
        ),
        [VM, VM, VM, SM, SM, SM, SM],
        [VM, VM, VM, SM],
        scratch=[pltpu.VMEM((TILES, 128), f32)],
    )(ref_pos, displacement, m, lists, row_tiles, column_tiles, bond_count)

    def sel(n):
        return pltpu.VMEM((KROWS, 128 * n), bf16)

    from_low, from_high = swap(low, high, "slab")
    bits, acc, tall, sel_phi = call(
        functools.partial(local_stretch_kernel, 0),
        "stretch_a",
        (
            shape(SLOTS + 1, 16, 128, dtype=i32),
            shape(TILES, 128),
            shape(TILES, 128, KROWS, dtype=bf16),
            shape(16, 128, 128, dtype=bf16),
        ),
        [SM, VM, VM, VM],
        scratch=[sel(6)],
        flops=1 << 26,
    )(meta, table, masks, broken)
    side = [
        jnp.concatenate(
            [part[t * GHOST : (t + 1) * GHOST] for part in (from_low, low, high, from_high)], 0
        )
        for t in range(2)
    ]
    left, right = swap(side[0], side[1], "thick")
    (acc,) = call(
        functools.partial(local_stretch_kernel, 1),
        "stretch_b",
        (shape(TILES, 128),),
        [SM] + [VM] * 4,
        aliases={4: 0},
        scratch=[sel(6)],
        flops=1 << 26,
    )(meta, table, bits, tall, acc)

    acc, ghosts, to_left, to_right, middle = call(
        ghost_stretch_kernel,
        "ghost_stretch",
        (
            shape(TILES, 128),
            shape(CELLS * GHOST, 8, 128),
            shape(4, GHOST, 128),
            shape(4, GHOST, 128),
            shape(4, GHOST, 128),
        ),
        [SM] + [VM] * 7,
        aliases={7: 0},
        scratch=[pltpu.VMEM((CELLS * GHOST, 128), f32), sel(6)],
    )(meta, tall, bits, from_low, from_high, left, right, acc)

    back_left, back_right = swap(to_left, to_right, "thick")
    terms = call(
        functools.partial(ghost_terms_kernel, 0),
        "ghost_terms_a",
        (shape(TILES, 8, 128), shape(CELLS * GHOST, 8, 128)),
        [SM, VM, VM, VM],
        scratch=[sel(7)],
        flops=1 << 26,
    )(meta, tall, ghosts, bits)
    to_low = jnp.stack([middle[0] + back_left[0], middle[1] + back_right[0]], 0)
    to_high = jnp.stack([middle[2] + back_left[3], middle[3] + back_right[3]], 0)
    back_low, back_high = swap(to_low, to_high, "slab")
    row_terms, column_terms = call(
        functools.partial(ghost_terms_kernel, 1),
        "ghost_terms_b",
        (shape(TILES, 8, 128), shape(CELLS * GHOST, 8, 128)),
        [SM] + [VM] * 5,
        aliases={4: 0, 5: 1},
        scratch=[sel(7)],
        flops=1 << 26,
    )(meta, tall, ghosts, bits, *terms)

    unused, table, tall_phi, dilatation, to_left, to_right, middle = call(
        dilatation_kernel,
        "dilatation",
        (
            shape(CELLS * GHOST, 8, 128),
            shape(TILES, 8, 128),
            shape(8, 128, 128, dtype=bf16),
            shape(TILES, 128),
            shape(4 * GHOST, 8, 128),
            shape(4 * GHOST, 8, 128),
            shape(4 * GHOST, 8, 128),
        ),
        [SM, SM] + [VM] * 12,
        aliases={13: 0, 2: 1},
        scratch=[pltpu.VMEM((TILES, 128), f32), pltpu.VMEM((TILES, 8, 128), f32), sel(3)],
    )(
        meta, lists, table, tall, sel_phi, ghosts, bits, acc, m, back_left, back_right, back_low,
        back_high, column_terms,
    )

    from_left, from_right = swap(to_left, to_right, "thick")
    (local,) = call(
        functools.partial(local_force_kernel, 0),
        "force_a",
        (shape(TILES, 8, 128),),
        [SM] + [VM] * 5,
        scratch=[sel(7)],
        flops=1 << 26,
    )(meta, table, tall, tall_phi, sel_phi, bits)
    to_low, to_high = call(
        relay_kernel,
        "relay",
        (shape(2 * GHOST, 8, 128), shape(2 * GHOST, 8, 128)),
        [VM] * 3,
    )(from_left, from_right, middle)
    from_low, from_high = swap(to_low, to_high, "slab")
    (local,) = call(
        functools.partial(local_force_kernel, 1),
        "force_b",
        (shape(TILES, 8, 128),),
        [SM] + [VM] * 6,
        aliases={6: 0},
        scratch=[sel(7)],
        flops=1 << 26,
    )(meta, table, tall, tall_phi, sel_phi, bits, local)
    (force,) = call(
        force_kernel,
        "force",
        (shape(3, TILES * 128),),
        [SM, SM] + [VM] * 12,
        scratch=[
            pltpu.VMEM((TILES, 8, 128), f32),
            sel(3),
            pltpu.VMEM((CELLS * GHOST, 128), f32),
        ],
    )(
        meta, lists, table, tall, tall_phi, sel_phi, ghosts, bits, local, row_terms, from_left,
        from_right, from_low, from_high,
    )
    return force, dilatation.reshape(TILES * 128)


def solution(mesh):
    in_specs = (
        P(None, ("slab", "thick")),
        P(None, ("slab", "thick")),
        P(("slab", "thick")),
        P(None, None, ("slab", "thick")),
        P(("slab", "thick")),
        P(("slab", "thick")),
        P(("slab", "thick")),
        P(("slab", "thick"), None, None),
        P(("slab", "thick"), None, None),
    )
    out_specs = (P(None, ("slab", "thick")), P(("slab", "thick")))
    return jax.shard_map(body, mesh=mesh, in_specs=in_specs, out_specs=out_specs, check_vma=False)
```

```python
import functools

import jax
import jax.numpy as jnp
from jax import lax
from jax.experimental import pallas as pl
from jax.experimental.pallas import tpu as pltpu
from jax.sharding import PartitionSpec as P

young = 25.0
poisson = 0.22
bulk_modulus = young / (3.0 * (1.0 - 2.0 * poisson))
shear_modulus = young / (2.0 * (1.0 + poisson))
volumetric_term = 3.0 * bulk_modulus - 5.0 * shear_modulus
shear_term = 15.0 * shear_modulus
radius_floor = 0.5
floor_squared = radius_floor * radius_floor

TILES = 128
SLOTS = 128
GHOST = 16
CELLS = 12
LISTS = 4 * GHOST
GROUP = 4
DUMMIES = 3 * GROUP
GHOST_AT = 144
COUNT_AT = 288
META = 296

f32 = jnp.float32
bf16 = jnp.bfloat16
PARTS = 32
i32 = jnp.int32
VM = pl.BlockSpec(memory_space=pltpu.VMEM)
SM = pl.BlockSpec(memory_space=pltpu.SMEM)
ANY = pl.BlockSpec(memory_space=pl.ANY)
HBM = pl.BlockSpec(memory_space=pltpu.HBM)


def shape(*dims, dtype=f32):
    return jax.ShapeDtypeStruct(dims, dtype)


def call(kernel, name, outs, ins, out_spaces=None, aliases=None, scratch=(), flops=0):
    def run(*args):
        return pl.pallas_call(
            kernel,
            out_shape=outs,
            in_specs=list(ins),
            out_specs=list(out_spaces or [VM] * len(outs)),
            scratch_shapes=list(scratch),
            input_output_aliases=aliases or {},
            compiler_params=pltpu.CompilerParams(vmem_limit_bytes=24 << 20),
            cost_estimate=pl.CostEstimate(flops=flops, bytes_accessed=1 << 20, transcendentals=0),
            name=name,
        )(*args)

    return run


def bcast_row(row):
    return jnp.broadcast_to(row, (8, 128))


def lane(column):
    return jnp.broadcast_to(column, (8, 128))


def fold(block):
    return jnp.sum(block, axis=0, keepdims=True)


def listed(lists):
    for s in range(2):
        for t in range(2):
            for g in range(GHOST):
                yield (2 * s + t) * GHOST + g, lists[s, t, g], g, s, t


def decode(code):
    return code & 255, (code >> 8) & 255, code >> 16


def over_slots(meta, base, count, half, spread, use, bufs):
    total = lax.div(count + (2 * GROUP - 1), 2 * GROUP)
    mid = lax.div(total + 1, 2)
    lo, hi = {None: (0, total), 0: (0, mid), 1: (mid, total)}[half]

    def ahead(group, buf):
        for i in range(GROUP):
            spread(*decode(meta[base + group * GROUP + i]), buf.at[i])

    def work(group, buf):
        for i in range(GROUP):
            use(*decode(meta[base + group * GROUP + i]), buf.at[i])

    ahead(2 * lo, bufs.at[0])

    def step(i, carry):
        ahead(2 * i + 1, bufs.at[1])
        work(2 * i, bufs.at[0])
        ahead(2 * i + 2, bufs.at[0])
        work(2 * i + 1, bufs.at[1])
        return carry

    lax.fori_loop(lo, hi, step, 0)


def bit_mask(bits, k, w, probe):
    return (bcast_row(bits[k, w : w + 1, :]) & probe) != 0


def probe_bits():
    return jnp.left_shift(jnp.int32(1), lax.broadcasted_iota(i32, (8, 128), 0))


def pack_kernel(
    x_in, u_in, m_in, lists_in, rows_in, cols_in, count_in, table, low, high, meta, lists, x, u, m,
    rows, cols, count, sems,
):
    pairs = (
        (x_in, x), (u_in, u), (m_in, m), (lists_in, lists), (rows_in, rows), (cols_in, cols),
        (count_in, count),
    )
    copies = [pltpu.make_async_copy(a, b, sems.at[n]) for n, (a, b) in enumerate(pairs)]
    for copy in copies:
        copy.start()
    for copy in copies:
        copy.wait()
    m[...] = shear_term / m[...]
    zero = jnp.zeros((1, 128), f32)

    def tile(t, carry):
        at = pl.ds(pl.multiple_of(t * 128, 128), 128)
        table[t, 0:3, :] = x[:, at]
        table[t, 3:6, :] = u[:, at]
        table[t, 6:7, :] = m[pl.ds(t, 1), :]
        table[t, 7:8, :] = zero
        return carry

    lax.fori_loop(0, TILES, tile, 0, unroll=8)
    for side, out in ((0, low), (1, high)):
        for g in range(2 * GHOST):
            out[g] = table[lists[side, g // GHOST, g % GHOST]]

    def sort(k, carry):
        nl, ng = carry
        b = cols[k]
        code = k + rows[k] * 256 + b * 65536
        ghost = (b >= TILES).astype(i32)
        meta[nl] = code
        meta[GHOST_AT + ng] = code
        return nl + 1 - ghost, ng + ghost

    nl, ng = lax.fori_loop(0, count[0], sort, (jnp.int32(0), jnp.int32(0)))
    for n in range(DUMMIES):
        meta[nl + n] = SLOTS
        meta[GHOST_AT + ng + n] = SLOTS + TILES * 65536
    meta[COUNT_AT] = nl
    meta[COUNT_AT + 1] = ng


def split3(v):
    hi = v.astype(bf16).astype(f32)
    rest = v - hi
    mid = rest.astype(bf16).astype(f32)
    return hi, mid, rest - mid


def parts_of(block):
    return jnp.concatenate(list(split3(block)) + [jnp.zeros((8, 128), f32)], 0)


XY = tuple((c,) for c in range(3)) + tuple((c, 3 + c) for c in range(3))
Y = XY[3:]
STIFF = (6,)


def selector(blocks, own):
    wide = 128 * len(blocks)
    row = lax.broadcasted_iota(i32, (PARTS, wide), 0)
    c = row & 7
    n = lax.broadcasted_iota(i32, (PARTS, wide), 1) >> 7
    out = jnp.zeros((PARTS, wide), f32)
    for at, names in enumerate(blocks):
        for name in names:
            value = -1.0 if own and name != 6 else 1.0
            out = jnp.where((n == at) & (c == name) & (row < 24), value, out)
    return out.astype(bf16)


def pair_values(tall, a, other, b, sel):
    count = sel.shape[1] // 128
    theirs = other[b]
    right = jnp.concatenate([theirs] * count, 1) * sel[PARTS:, :]
    return jnp.dot(
        tall[a], jnp.concatenate([sel[0:PARTS, :], right], 0), preferred_element_type=f32
    )


def fill(sel, blocks):
    sel[0:PARTS, :] = selector(blocks, True)
    sel[PARTS:, :] = selector(blocks, False)


def spread_phi(tall_phi, sel_phi, a):
    return jnp.dot(tall_phi[a >> 4], sel_phi[a & 15], preferred_element_type=f32)


def piece(rows, w, c):
    return rows[8 * w : 8 * w + 8, 128 * c : 128 * c + 128]


def length2(v):
    return jnp.maximum(v[0] * v[0] + v[1] * v[1] + v[2] * v[2], floor_squared)


def bond(rows, w):
    r2 = length2([piece(rows, w, c) for c in range(3)])
    y = [piece(rows, w, 3 + c) for c in range(3)]
    s2 = length2(y)
    return y, r2, s2, lax.rsqrt(r2), lax.rsqrt(s2)


def unit(rows, w):
    y = [piece(rows, w, c) for c in range(3)]
    return y, lax.rsqrt(length2(y))


def lane_sum(block):
    return jnp.sum(block, axis=1, keepdims=True)


def merge3(parts):
    lan = lax.broadcasted_iota(i32, (8, 128), 1)
    return jnp.where(lan == 0, lane(parts[0]), jnp.where(lan == 1, lane(parts[1]), lane(parts[2])))


def stretch_slot(tall, sel, other, base, bits, probe, row_acc, col_acc):
    def spread(k, a, b, rows):
        rows[...] = pair_values(tall, a, other, b - base, sel)

    def use(k, a, b, rows):
        bb = b - base
        down = None
        across = []
        for w in range(16):
            y, r2, s2, rinv, sinv = bond(rows, w)
            e = s2 * sinv - r2 * rinv
            e = jnp.where(bit_mask(bits, k, w, probe), e, 0.0)
            down = e if down is None else down + e
            across.append(lane(lane_sum(e)))
        sums = jnp.transpose(jnp.concatenate(across, 0))[0:1, :]
        row_acc[pl.ds(a, 1), :] += sums
        col_acc[pl.ds(bb, 1), :] += fold(down)

    return spread, use


def local_stretch_kernel(half, meta, *refs):
    if half == 0:
        tab, masks_in, broken_in, bits, acc, tall, wide, sel_phi, sel, masks, broken, sems, bufs = refs
        copies = [
            pltpu.make_async_copy(masks_in, masks, sems.at[0]),
            pltpu.make_async_copy(broken_in, broken, sems.at[1]),
        ]
        for copy in copies:
            copy.start()
        acc[...] = jnp.zeros_like(acc)
        ones = jnp.ones((PARTS, 128), bf16)

        def stand(t, carry):
            parts = parts_of(tab[t]).astype(bf16)
            wide[t] = parts
            tall[t] = jnp.transpose(jnp.concatenate([parts, ones], 0))
            return carry

        lax.fori_loop(0, TILES, stand, 0, unroll=8)
        k = lax.broadcasted_iota(i32, (128, 128), 0)
        for n in range(16):
            sel_phi[n] = jnp.where(((k >> 3) == n) & ((k & 7) < 3), 1.0, 0.0).astype(bf16)
        for copy in copies:
            copy.wait()

        def clear(k, carry):
            bits[k] = masks[k] & ~broken[k]
            return carry

        lax.fori_loop(0, SLOTS, clear, 0, unroll=8)
        bits[SLOTS] = jnp.zeros((16, 128), i32)
        w = lax.broadcasted_iota(i32, (16, 128), 0)
        j = lax.broadcasted_iota(i32, (16, 128), 1)
        below = jnp.zeros((16, 128), i32)
        for b in range(8):
            below += jnp.where(8 * w + b < j, 1 << b, 0)

        def own(i, carry):
            k, a, b = decode(meta[i])

            @pl.when(a == b)
            def _():
                bits[k] = bits[k] & below

            return carry

        lax.fori_loop(0, meta[COUNT_AT], own, 0)
    else:
        bits, tall, wide, unused, acc, sel, bufs = refs
    fill(sel, XY)
    over_slots(
        meta,
        0,
        meta[COUNT_AT],
        half,
        *stretch_slot(tall, sel, wide, 0, bits, probe_bits(), acc, acc),
        bufs,
    )


def side_kernel(from_low, low, high, from_high, after, to_left, to_right):
    for n, part in enumerate((from_low, low, high, from_high)):
        to_left[n * GHOST : (n + 1) * GHOST] = part[0:GHOST]
        to_right[n * GHOST : (n + 1) * GHOST] = part[GHOST:]


def row_of(cell):
    return cell // 4, cell % 4


cycle_cells = (0, 1, 2, 3, 4, 7, 8, 11, 12, 13, 14, 15)


def ghost_stretch_kernel(
    meta, tall, bits, low, high, left, right, unused, acc, ghosts, to_left, to_right, middle, gacc,
    sel, bufs,
):
    fill(sel, XY)
    for n, cell in enumerate(cycle_cells):
        r, c = row_of(cell)
        if c == 0:
            src, at = left, r * GHOST
        elif c == 3:
            src, at = right, r * GHOST
        else:
            src, at = (low if r == 0 else high), (c - 1) * GHOST
        for g in range(GHOST):
            ghosts[n * GHOST + g] = parts_of(src[at + g]).astype(bf16)
    gacc[...] = jnp.zeros_like(gacc)
    probe = probe_bits()
    over_slots(
        meta,
        GHOST_AT,
        meta[COUNT_AT + 1],
        None,
        *stretch_slot(tall, sel, ghosts, TILES, bits, probe, acc, gacc),
        bufs,
    )
    for n, cell in enumerate(cycle_cells):
        r, c = row_of(cell)
        part = gacc[n * GHOST : (n + 1) * GHOST, :]
        if c == 0:
            to_left[r] = part
        elif c == 3:
            to_right[r] = part
        else:
            middle[2 * (r // 3) + c - 1] = part


def middle_kernel(middle, left, right, after, to_low, to_high):
    for t, thick in ((0, left), (1, right)):
        to_low[t] = middle[t] + thick[0]
        to_high[t] = middle[2 + t] + thick[3]


def ghost_terms_kernel(half, meta, tall, ghosts, bits, *refs):
    if half == 0:
        rows_out, cols_out, sel, bufs = refs
        rows_out[...] = jnp.zeros_like(rows_out)
        cols_out[...] = jnp.zeros_like(cols_out)
    else:
        unused0, unused1, rows_out, cols_out, sel, bufs = refs
    fill(sel, XY + (STIFF,))
    probe = probe_bits()

    def spread(k, a, b, rows):
        rows[...] = pair_values(tall, a, ghosts, b - TILES, sel)

    def use(k, a, b, rows):
        bb = b - TILES
        down = [None] * 6
        across = []
        for w in range(16):
            y, r2, s2, rinv, sinv = bond(rows, w)
            g = (s2 * sinv * rinv - 1.0) * piece(rows, w, 6)
            keep = jnp.where(bit_mask(bits, k, w, probe), sinv, 0.0)
            v = [keep * y[c] for c in range(3)]
            p = [g * v[c] for c in range(3)]
            down = [q if d is None else d + q for d, q in zip(down, p + v)]
            across.append(merge3([lane_sum(q) for q in p]))
        sums = jnp.transpose(jnp.concatenate(across, 0))
        rows_out[a, 0:3, :] += sums[0:3, :]
        for c in range(6):
            cols_out[bb, c : c + 1, :] += fold(down[c])

    over_slots(meta, GHOST_AT, meta[COUNT_AT + 1], half, spread, use, bufs)


def dilatation_kernel(
    meta, lists, tab_in, tall, sel_phi, ghosts, bits, acc_in, m, from_left, from_right, from_low,
    from_high, terms_in, terms, tab, tall_phi, dil, to_left, to_right, middle, acc, parts, back, sel,
    bufs,
):
    acc[...] = acc_in[...]
    for s in range(2):
        for t in range(2):
            at = (2 * s + t) * GHOST
            back[at : at + GHOST, :] = (
                (from_left, from_right)[t][1 + s] + (from_low, from_high)[s][t]
            )
    for n, q, g, s, t in listed(lists):
        acc[pl.ds(q, 1), :] += back[n : n + 1, :]
    theta = 3.0 * acc[...] / m[...]
    dil[...] = theta
    acc[...] = volumetric_term * theta / m[...]

    parts[...] = jnp.zeros_like(parts)

    def tile(t, carry):
        phi = acc[pl.ds(t, 1), :]
        tab[t, 7:8, :] = phi
        for n, part in enumerate(split3(phi)):
            parts[t, n : n + 1, :] = part
        return carry

    lax.fori_loop(0, TILES, tile, 0, unroll=8)
    for n in range(8):
        block = parts[16 * n : 16 * n + 16].reshape(128, 128)
        tall_phi[n] = jnp.transpose(block).astype(bf16)
    fill(sel, Y)
    probe = probe_bits()

    def spread(k, a, b, rows):
        rows[:, 0:384] = pair_values(tall, a, ghosts, b - TILES, sel)
        rows[:, 384:] = spread_phi(tall_phi, sel_phi, a)

    def use(k, a, b, rows):
        bb = b - TILES
        down = [None] * 3
        for w in range(16):
            y, sinv = unit(rows, w)
            keep = jnp.where(bit_mask(bits, k, w, probe), sinv * piece(rows, w, 3), 0.0)
            v = [keep * y[c] for c in range(3)]
            down = [q if d is None else d + q for d, q in zip(down, v)]
        for c in range(3):
            terms[bb, c : c + 1, :] += fold(down[c])

    over_slots(meta, GHOST_AT, meta[COUNT_AT + 1], None, spread, use, bufs)
    for n, cell in enumerate(cycle_cells):
        r, c = row_of(cell)
        if c == 0:
            out, at = to_left, r * GHOST
        elif c == 3:
            out, at = to_right, r * GHOST
        else:
            out, at = middle, (2 * (r // 3) + c - 1) * GHOST
        out[at : at + GHOST] = terms[n * GHOST : (n + 1) * GHOST]
    for t, out in ((0, to_left), (1, to_right)):
        for s in range(2):
            for g in range(GHOST):
                phi = acc[pl.ds(lists[s, t, g], 1), :]
                out[s * GHOST + g, 6:7, :] = phi
                middle[(2 * s + t) * GHOST + g, 6:7, :] = phi


def relay_kernel(from_left, from_right, middle, after, to_low, to_high):
    thick = (from_left, from_right)
    for s, out in ((0, to_low), (1, to_high)):
        for t in range(2):
            for g in range(GHOST):
                n, at = t * GHOST + g, (2 * s + t) * GHOST + g
                far = thick[t][3 * s * GHOST + g]
                out[n, 0:6, :] = middle[at, 0:6, :] + far[0:6, :]
                out[n, 6:7, :] = middle[at, 6:7, :]
                out[n, 7:8, :] = thick[t][s * GHOST + g, 6:7, :]


def local_force_kernel(half, meta, tab, tall, wide, tall_phi, sel_phi, bits, *refs):
    if half == 0:
        acc, sel, bufs = refs
        acc[...] = jnp.zeros_like(acc)
    else:
        unused, acc, sel, bufs = refs
    fill(sel, XY + (STIFF,))
    probe = probe_bits()

    def spread(k, a, b, rows):
        rows[:, 0:896] = pair_values(tall, a, wide, b, sel)
        rows[:, 896:] = spread_phi(tall_phi, sel_phi, a)

    def use(k, a, b, rows):
        phi = bcast_row(tab[b, 7:8, :])
        down = [None] * 3
        across = []
        for w in range(16):
            y, r2, s2, rinv, sinv = bond(rows, w)
            g = (s2 * sinv * rinv - 1.0) * piece(rows, w, 6) + (phi + piece(rows, w, 7))
            keep = jnp.where(bit_mask(bits, k, w, probe), sinv * g, 0.0)
            v = [keep * y[c] for c in range(3)]
            down = [q if d is None else d + q for d, q in zip(down, v)]
            across.append(merge3([lane_sum(q) for q in v]))
        sums = jnp.transpose(jnp.concatenate(across, 0))
        acc[a, 0:3, :] += sums[0:3, :]
        for c in range(3):
            acc[b, c : c + 1, :] -= fold(down[c])

    over_slots(meta, 0, meta[COUNT_AT], half, spread, use, bufs)


def force_kernel(
    meta, lists, tab, tall, tall_phi, sel_phi, ghosts, bits, local, rows_in, from_left, from_right,
    from_low, from_high, force, acc, back, sel, gphi, bufs,
):
    for n, cell in enumerate(cycle_cells):
        r, c = row_of(cell)
        if r in (0, 3):
            src, at, line = (from_low if r == 0 else from_high), (c // 2) * GHOST, (7, 6, 6, 7)[c]
        else:
            src, at, line = (from_left if c == 0 else from_right), (r - 1) * GHOST, 6
        for g in range(GHOST):
            gphi[n * GHOST + g : n * GHOST + g + 1, :] = src[at + g, line : line + 1, :]

    acc[...] = local[...] + rows_in[...]
    fill(sel, Y)
    probe = probe_bits()

    def spread(k, a, b, rows):
        rows[:, 0:384] = pair_values(tall, a, ghosts, b - TILES, sel)
        rows[:, 384:] = spread_phi(tall_phi, sel_phi, a)

    def use(k, a, b, rows):
        bb = b - TILES
        phi = bcast_row(gphi[pl.ds(bb, 1), :])
        across = []
        for w in range(16):
            y, sinv = unit(rows, w)
            both = phi + piece(rows, w, 3)
            keep = jnp.where(bit_mask(bits, k, w, probe), sinv * both, 0.0)
            across.append(merge3([lane_sum(keep * y[c]) for c in range(3)]))
        sums = jnp.transpose(jnp.concatenate(across, 0))
        acc[a, 0:3, :] += sums[0:3, :]

    over_slots(meta, GHOST_AT, meta[COUNT_AT + 1], None, spread, use, bufs)
    for n, q, g, s, t in listed(lists):
        thick = (from_left, from_right)[t][(1 + s) * GHOST + g]
        both = thick + (from_low, from_high)[s][t * GHOST + g]
        back[n, 0:3, :] = both[0:3, :] + tab[q, 7:8, :] * both[3:6, :]
    for n, q, g, s, t in listed(lists):
        acc[q, 0:3, :] -= back[n, 0:3, :]

    def store(t, carry):
        force[:, pl.ds(pl.multiple_of(t * 128, 128), 128)] = acc[t, 0:3, :]
        return carry

    lax.fori_loop(0, TILES, store, 0, unroll=8)


def shifts(axis):
    count = lax.axis_size(axis)
    forward = [(i, i + 1) for i in range(count - 1)]
    return forward, [(target, source) for source, target in forward]


def swap(to_low, to_high, axis):
    forward, backward = shifts(axis)
    return lax.ppermute(to_high, axis, forward), lax.ppermute(to_low, axis, backward)


def body(
    ref_pos, displacement, weighted_volume, corner_lists, row_tiles, column_tiles, bond_count,
    masks, broken,
):
    m = weighted_volume.reshape(TILES, 128)
    table, low, high, meta, lists = call(
        pack_kernel,
        "pack",
        (
            shape(TILES, 8, 128),
            shape(2 * GHOST, 8, 128),
            shape(2 * GHOST, 8, 128),
            shape(META, dtype=i32),
            shape(2, 2, GHOST, dtype=i32),
        ),
        [HBM] * 7,
        [VM, VM, VM, SM, SM],
        scratch=[
            pltpu.VMEM((3, TILES * 128), f32),
            pltpu.VMEM((3, TILES * 128), f32),
            pltpu.VMEM((TILES, 128), f32),
            pltpu.SMEM((SLOTS,), i32),
            pltpu.SMEM((SLOTS,), i32),
            pltpu.SMEM((1,), i32),
            pltpu.SemaphoreType.DMA((7,)),
        ],
    )(ref_pos, displacement, m, corner_lists, row_tiles, column_tiles, bond_count)

    def sel(n):
        return pltpu.VMEM((2 * PARTS, 128 * n), bf16)

    def bufs(n):
        return pltpu.VMEM((2, GROUP, 128, 128 * n), f32)

    from_low, from_high = swap(low, high, "slab")
    bits, acc, tall, wide, sel_phi = call(
        functools.partial(local_stretch_kernel, 0),
        "stretch_a",
        (
            shape(SLOTS + 1, 16, 128, dtype=i32),
            shape(TILES, 128),
            shape(TILES, 128, 2 * PARTS, dtype=bf16),
            shape(TILES, PARTS, 128, dtype=bf16),
            shape(16, 128, 128, dtype=bf16),
        ),
        [SM, VM, HBM, HBM],
        scratch=[
            sel(6),
            pltpu.VMEM((SLOTS, 16, 128), i32),
            pltpu.VMEM((SLOTS, 16, 128), i32),
            pltpu.SemaphoreType.DMA((2,)),
            bufs(6),
        ],
        flops=1 << 26,
    )(meta, table, masks, broken)
    side = call(
        side_kernel,
        "side",
        (shape(4 * GHOST, 8, 128), shape(4 * GHOST, 8, 128)),
        [VM] * 4 + [ANY],
    )(from_low, low, high, from_high, acc)
    left, right = swap(side[0], side[1], "thick")
    (acc,) = call(
        functools.partial(local_stretch_kernel, 1),
        "stretch_b",
        (shape(TILES, 128),),
        [SM] + [VM] * 4,
        aliases={4: 0},
        scratch=[sel(6), bufs(6)],
        flops=1 << 26,
    )(meta, bits, tall, wide, acc)

    acc, ghosts, to_left, to_right, middle = call(
        ghost_stretch_kernel,
        "ghost_stretch",
        (
            shape(TILES, 128),
            shape(CELLS * GHOST, PARTS, 128, dtype=bf16),
            shape(4, GHOST, 128),
            shape(4, GHOST, 128),
            shape(4, GHOST, 128),
        ),
        [SM] + [VM] * 7,
        aliases={7: 0},
        scratch=[pltpu.VMEM((CELLS * GHOST, 128), f32), sel(6), bufs(6)],
    )(meta, tall, bits, from_low, from_high, left, right, acc)

    back_left, back_right = swap(to_left, to_right, "thick")
    terms = call(
        functools.partial(ghost_terms_kernel, 0),
        "ghost_terms_a",
        (shape(TILES, 8, 128), shape(CELLS * GHOST, 8, 128)),
        [SM, VM, VM, VM],
        scratch=[sel(7), bufs(7)],
        flops=1 << 26,
    )(meta, tall, ghosts, bits)
    to_low, to_high = call(
        middle_kernel,
        "middle",
        (shape(2, GHOST, 128), shape(2, GHOST, 128)),
        [VM] * 3 + [ANY],
    )(middle, back_left, back_right, terms[0])
    back_low, back_high = swap(to_low, to_high, "slab")
    row_terms, column_terms = call(
        functools.partial(ghost_terms_kernel, 1),
        "ghost_terms_b",
        (shape(TILES, 8, 128), shape(CELLS * GHOST, 8, 128)),
        [SM] + [VM] * 5,
        aliases={4: 0, 5: 1},
        scratch=[sel(7), bufs(7)],
        flops=1 << 26,
    )(meta, tall, ghosts, bits, *terms)

    unused, table, tall_phi, dilatation, to_left, to_right, middle = call(
        dilatation_kernel,
        "dilatation",
        (
            shape(CELLS * GHOST, 8, 128),
            shape(TILES, 8, 128),
            shape(8, 128, 128, dtype=bf16),
            shape(TILES, 128),
            shape(4 * GHOST, 8, 128),
            shape(4 * GHOST, 8, 128),
            shape(4 * GHOST, 8, 128),
        ),
        [SM, SM] + [VM] * 12,
        aliases={13: 0, 2: 1},
        scratch=[
            pltpu.VMEM((TILES, 128), f32),
            pltpu.VMEM((TILES, 8, 128), f32),
            pltpu.VMEM((LISTS, 128), f32),
            sel(3),
            bufs(4),
        ],
    )(
        meta, lists, table, tall, sel_phi, ghosts, bits, acc, m, back_left, back_right, back_low,
        back_high, column_terms,
    )

    from_left, from_right = swap(to_left, to_right, "thick")
    (local,) = call(
        functools.partial(local_force_kernel, 0),
        "force_a",
        (shape(TILES, 8, 128),),
        [SM] + [VM] * 6,
        scratch=[sel(7), bufs(8)],
        flops=1 << 26,
    )(meta, table, tall, wide, tall_phi, sel_phi, bits)
    to_low, to_high = call(
        relay_kernel,
        "relay",
        (shape(2 * GHOST, 8, 128), shape(2 * GHOST, 8, 128)),
        [VM] * 3 + [ANY],
    )(from_left, from_right, middle, local)
    from_low, from_high = swap(to_low, to_high, "slab")
    (local,) = call(
        functools.partial(local_force_kernel, 1),
        "force_b",
        (shape(TILES, 8, 128),),
        [SM] + [VM] * 7,
        aliases={7: 0},
        scratch=[sel(7), bufs(8)],
        flops=1 << 26,
    )(meta, table, tall, wide, tall_phi, sel_phi, bits, local)
    (force,) = call(
        force_kernel,
        "force",
        (shape(3, TILES * 128),),
        [SM, SM] + [VM] * 12,
        scratch=[
            pltpu.VMEM((TILES, 8, 128), f32),
            pltpu.VMEM((LISTS, 8, 128), f32),
            sel(3),
            pltpu.VMEM((CELLS * GHOST, 128), f32),
            bufs(4),
        ],
    )(
        meta, lists, table, tall, tall_phi, sel_phi, ghosts, bits, local, row_terms, from_left,
        from_right, from_low, from_high,
    )
    return force, dilatation.reshape(TILES * 128)


def solution(mesh):
    in_specs = (
        P(None, ("slab", "thick")),
        P(None, ("slab", "thick")),
        P(("slab", "thick")),
        P(None, None, ("slab", "thick")),
        P(("slab", "thick")),
        P(("slab", "thick")),
        P(("slab", "thick")),
        P(("slab", "thick"), None, None),
        P(("slab", "thick"), None, None),
    )
    out_specs = (P(None, ("slab", "thick")), P(("slab", "thick")))
    return jax.shard_map(body, mesh=mesh, in_specs=in_specs, out_specs=out_specs, check_vma=False)
```

```python
import functools

import jax
import jax.numpy as jnp
from jax import lax
from jax.experimental import pallas as pl
from jax.experimental.pallas import tpu as pltpu
from jax.sharding import PartitionSpec as P

young = 25.0
poisson = 0.22
bulk_modulus = young / (3.0 * (1.0 - 2.0 * poisson))
shear_modulus = young / (2.0 * (1.0 + poisson))
volumetric_term = 3.0 * bulk_modulus - 5.0 * shear_modulus
shear_term = 15.0 * shear_modulus
radius_floor = 0.5
floor_squared = radius_floor * radius_floor

TILES = 128
SLOTS = 128
GHOST = 16
CELLS = 12
LISTS = 4 * GHOST
GROUP = 4
DUMMIES = 3 * GROUP
GHOST_AT = 144
COUNT_AT = 288
META = 296

PACK_GRANT = 67043328 - (900 << 10)

f32 = jnp.float32
bf16 = jnp.bfloat16
PARTS = 32
i32 = jnp.int32
VM = pl.BlockSpec(memory_space=pltpu.VMEM)
SM = pl.BlockSpec(memory_space=pltpu.SMEM)
ANY = pl.BlockSpec(memory_space=pl.ANY)
HBM = pl.BlockSpec(memory_space=pltpu.HBM)


def shape(*dims, dtype=f32):
    return jax.ShapeDtypeStruct(dims, dtype)


def call(
    kernel, name, outs, ins, out_spaces=None, aliases=None, scratch=(), flops=0, grant=24 << 20
):
    def run(*args):
        return pl.pallas_call(
            kernel,
            out_shape=outs,
            in_specs=list(ins),
            out_specs=list(out_spaces or [VM] * len(outs)),
            scratch_shapes=list(scratch),
            input_output_aliases=aliases or {},
            compiler_params=pltpu.CompilerParams(
                vmem_limit_bytes=grant,
            ),
            cost_estimate=pl.CostEstimate(flops=flops, bytes_accessed=1 << 20, transcendentals=0),
            name=name,
        )(*args)

    return run


def bcast_row(row):
    return jnp.broadcast_to(row, (8, 128))


def lane(column):
    return jnp.broadcast_to(column, (8, 128))


def fold(block):
    return jnp.sum(block, axis=0, keepdims=True)


def listed(lists):
    for s in range(2):
        for t in range(2):
            for g in range(GHOST):
                yield (2 * s + t) * GHOST + g, lists[s, t, g], g, s, t


def decode(code):
    return code & 255, (code >> 8) & 255, code >> 16


def over_slots(meta, base, count, half, spread, use, bufs):
    total = lax.div(count + (2 * GROUP - 1), 2 * GROUP)
    mid = lax.div(total + 1, 2)
    lo, hi = {None: (0, total), 0: (0, mid), 1: (mid, total)}[half]

    def ahead(group, buf):
        for i in range(GROUP):
            spread(*decode(meta[base + group * GROUP + i]), buf.at[i])

    def work(group, buf):
        for i in range(GROUP):
            use(*decode(meta[base + group * GROUP + i]), buf.at[i])

    ahead(2 * lo, bufs.at[0])

    def step(i, carry):
        ahead(2 * i + 1, bufs.at[1])
        work(2 * i, bufs.at[0])
        ahead(2 * i + 2, bufs.at[0])
        work(2 * i + 1, bufs.at[1])
        return carry

    lax.fori_loop(lo, hi, step, 0)


def bit_mask(bits, k, w, probe):
    return (bcast_row(bits[k, w : w + 1, :]) & probe) != 0


def probe_bits():
    return jnp.left_shift(jnp.int32(1), lax.broadcasted_iota(i32, (8, 128), 0))


def pack_kernel(
    x_in, u_in, m_in, lists_in, rows_in, cols_in, count_in, table, low, high, meta, lists, x, u, m,
    rows, cols, count, sems,
):
    pairs = (
        (x_in, x), (u_in, u), (m_in, m), (lists_in, lists), (rows_in, rows), (cols_in, cols),
        (count_in, count),
    )
    copies = [pltpu.make_async_copy(a, b, sems.at[n]) for n, (a, b) in enumerate(pairs)]
    for copy in copies:
        copy.start()
    for copy in copies:
        copy.wait()
    m[...] = shear_term / m[...]
    zero = jnp.zeros((1, 128), f32)

    def tile(t, carry):
        at = pl.ds(pl.multiple_of(t * 128, 128), 128)
        table[t, 0:3, :] = x[:, at]
        table[t, 3:6, :] = u[:, at]
        table[t, 6:7, :] = m[pl.ds(t, 1), :]
        table[t, 7:8, :] = zero
        return carry

    lax.fori_loop(0, TILES, tile, 0, unroll=8)
    for side, out in ((0, low), (1, high)):
        for g in range(2 * GHOST):
            out[g] = table[lists[side, g // GHOST, g % GHOST]]

    def sort(k, carry):
        nl, ng = carry
        b = cols[k]
        code = k + rows[k] * 256 + b * 65536
        ghost = (b >= TILES).astype(i32)
        meta[nl] = code
        meta[GHOST_AT + ng] = code
        return nl + 1 - ghost, ng + ghost

    nl, ng = lax.fori_loop(0, count[0], sort, (jnp.int32(0), jnp.int32(0)))
    for n in range(DUMMIES):
        meta[nl + n] = SLOTS
        meta[GHOST_AT + ng + n] = SLOTS + TILES * 65536
    meta[COUNT_AT] = nl
    meta[COUNT_AT + 1] = ng


def split3(v):
    hi = v.astype(bf16).astype(f32)
    rest = v - hi
    mid = rest.astype(bf16).astype(f32)
    return hi, mid, rest - mid


def parts_of(block):
    return jnp.concatenate(list(split3(block)) + [jnp.zeros((8, 128), f32)], 0)


XY = tuple((c,) for c in range(3)) + tuple((c, 3 + c) for c in range(3))
Y = XY[3:]
STIFF = (6,)


def selector(blocks, own):
    wide = 128 * len(blocks)
    row = lax.broadcasted_iota(i32, (PARTS, wide), 0)
    c = row & 7
    n = lax.broadcasted_iota(i32, (PARTS, wide), 1) >> 7
    out = jnp.zeros((PARTS, wide), f32)
    for at, names in enumerate(blocks):
        for name in names:
            value = -1.0 if own and name != 6 else 1.0
            out = jnp.where((n == at) & (c == name) & (row < 24), value, out)
    return out.astype(bf16)


def pair_values(tall, a, other, b, sel):
    count = sel.shape[1] // 128
    theirs = other[b]
    right = jnp.concatenate([theirs] * count, 1) * sel[PARTS:, :]
    return jnp.dot(
        tall[a], jnp.concatenate([sel[0:PARTS, :], right], 0), preferred_element_type=f32
    )


def fill(sel, blocks):
    sel[0:PARTS, :] = selector(blocks, True)
    sel[PARTS:, :] = selector(blocks, False)


def spread_phi(tall_phi, sel_phi, a):
    return jnp.dot(tall_phi[a >> 4], sel_phi[a & 15], preferred_element_type=f32)


def piece(rows, w, c):
    return rows[8 * w : 8 * w + 8, 128 * c : 128 * c + 128]


def length2(v):
    return jnp.maximum(v[0] * v[0] + v[1] * v[1] + v[2] * v[2], floor_squared)


def bond(rows, w):
    r2 = length2([piece(rows, w, c) for c in range(3)])
    y = [piece(rows, w, 3 + c) for c in range(3)]
    s2 = length2(y)
    return y, r2, s2, lax.rsqrt(r2), lax.rsqrt(s2)


def unit(rows, w):
    y = [piece(rows, w, c) for c in range(3)]
    return y, lax.rsqrt(length2(y))


def lane_sum(block):
    return jnp.sum(block, axis=1, keepdims=True)


def merge3(parts):
    lan = lax.broadcasted_iota(i32, (8, 128), 1)
    return jnp.where(lan == 0, lane(parts[0]), jnp.where(lan == 1, lane(parts[1]), lane(parts[2])))


def stretch_slot(tall, sel, other, base, bits, probe, row_acc, col_acc):
    def spread(k, a, b, rows):
        rows[...] = pair_values(tall, a, other, b - base, sel)

    def use(k, a, b, rows):
        bb = b - base
        down = None
        across = []
        for w in range(16):
            y, r2, s2, rinv, sinv = bond(rows, w)
            e = s2 * sinv - r2 * rinv
            e = jnp.where(bit_mask(bits, k, w, probe), e, 0.0)
            down = e if down is None else down + e
            across.append(lane(lane_sum(e)))
        sums = jnp.transpose(jnp.concatenate(across, 0))[0:1, :]
        row_acc[pl.ds(a, 1), :] += sums
        col_acc[pl.ds(bb, 1), :] += fold(down)

    return spread, use


def local_stretch_kernel(half, meta, *refs):
    if half == 0:
        tab, unused, bits, acc, tall, wide, sel_phi, sel, bufs = refs
        acc[...] = jnp.zeros_like(acc)
        ones = jnp.ones((PARTS, 128), bf16)

        def stand(t, carry):
            parts = parts_of(tab[t]).astype(bf16)
            wide[t] = parts
            tall[t] = jnp.transpose(jnp.concatenate([parts, ones], 0))
            return carry

        lax.fori_loop(0, TILES, stand, 0, unroll=8)
        k = lax.broadcasted_iota(i32, (128, 128), 0)
        for n in range(16):
            sel_phi[n] = jnp.where(((k >> 3) == n) & ((k & 7) < 3), 1.0, 0.0).astype(bf16)
        w = lax.broadcasted_iota(i32, (16, 128), 0)
        j = lax.broadcasted_iota(i32, (16, 128), 1)
        below = jnp.zeros((16, 128), i32)
        for b in range(8):
            below += jnp.where(8 * w + b < j, 1 << b, 0)

        def own(i, carry):
            k, a, b = decode(meta[i])

            @pl.when(a == b)
            def _():
                bits[k] = bits[k] & below

            return carry

        lax.fori_loop(0, meta[COUNT_AT], own, 0)
    else:
        bits, tall, wide, unused, acc, sel, bufs = refs
    fill(sel, XY)
    over_slots(
        meta,
        0,
        meta[COUNT_AT],
        half,
        *stretch_slot(tall, sel, wide, 0, bits, probe_bits(), acc, acc),
        bufs,
    )


def side_kernel(from_low, low, high, from_high, after, to_left, to_right):
    for n, part in enumerate((from_low, low, high, from_high)):
        to_left[n * GHOST : (n + 1) * GHOST] = part[0:GHOST]
        to_right[n * GHOST : (n + 1) * GHOST] = part[GHOST:]


def row_of(cell):
    return cell // 4, cell % 4


cycle_cells = (0, 1, 2, 3, 4, 7, 8, 11, 12, 13, 14, 15)


def ghost_stretch_kernel(
    meta, tall, bits, low, high, left, right, unused, acc, ghosts, to_left, to_right, middle, gacc,
    sel, bufs,
):
    fill(sel, XY)
    for n, cell in enumerate(cycle_cells):
        r, c = row_of(cell)
        if c == 0:
            src, at = left, r * GHOST
        elif c == 3:
            src, at = right, r * GHOST
        else:
            src, at = (low if r == 0 else high), (c - 1) * GHOST
        for g in range(GHOST):
            ghosts[n * GHOST + g] = parts_of(src[at + g]).astype(bf16)
    gacc[...] = jnp.zeros_like(gacc)
    probe = probe_bits()
    over_slots(
        meta,
        GHOST_AT,
        meta[COUNT_AT + 1],
        None,
        *stretch_slot(tall, sel, ghosts, TILES, bits, probe, acc, gacc),
        bufs,
    )
    for n, cell in enumerate(cycle_cells):
        r, c = row_of(cell)
        part = gacc[n * GHOST : (n + 1) * GHOST, :]
        if c == 0:
            to_left[r] = part
        elif c == 3:
            to_right[r] = part
        else:
            middle[2 * (r // 3) + c - 1] = part


def middle_kernel(middle, left, right, after, to_low, to_high):
    for t, thick in ((0, left), (1, right)):
        to_low[t] = middle[t] + thick[0]
        to_high[t] = middle[2 + t] + thick[3]


def ghost_terms_kernel(half, meta, tall, ghosts, bits, *refs):
    if half == 0:
        rows_out, cols_out, sel, bufs = refs
        rows_out[...] = jnp.zeros_like(rows_out)
        cols_out[...] = jnp.zeros_like(cols_out)
    else:
        unused0, unused1, rows_out, cols_out, sel, bufs = refs
    fill(sel, XY + (STIFF,))
    probe = probe_bits()

    def spread(k, a, b, rows):
        rows[...] = pair_values(tall, a, ghosts, b - TILES, sel)

    def use(k, a, b, rows):
        bb = b - TILES
        down = [None] * 6
        across = []
        for w in range(16):
            y, r2, s2, rinv, sinv = bond(rows, w)
            g = (s2 * sinv * rinv - 1.0) * piece(rows, w, 6)
            keep = jnp.where(bit_mask(bits, k, w, probe), sinv, 0.0)
            v = [keep * y[c] for c in range(3)]
            p = [g * v[c] for c in range(3)]
            down = [q if d is None else d + q for d, q in zip(down, p + v)]
            across.append(merge3([lane_sum(q) for q in p]))
        sums = jnp.transpose(jnp.concatenate(across, 0))
        rows_out[a, 0:3, :] += sums[0:3, :]
        for c in range(6):
            cols_out[bb, c : c + 1, :] += fold(down[c])

    over_slots(meta, GHOST_AT, meta[COUNT_AT + 1], half, spread, use, bufs)


def dilatation_kernel(
    meta, lists, tab_in, tall, sel_phi, ghosts, bits, acc_in, m, from_left, from_right, from_low,
    from_high, terms_in, terms, tab, tall_phi, dil, to_left, to_right, middle, acc, parts, back, sel,
    bufs,
):
    acc[...] = acc_in[...]
    for s in range(2):
        for t in range(2):
            at = (2 * s + t) * GHOST
            back[at : at + GHOST, :] = (
                (from_left, from_right)[t][1 + s] + (from_low, from_high)[s][t]
            )
    for n, q, g, s, t in listed(lists):
        acc[pl.ds(q, 1), :] += back[n : n + 1, :]
    theta = 3.0 * acc[...] / m[...]
    dil[...] = theta
    acc[...] = volumetric_term * theta / m[...]

    parts[...] = jnp.zeros_like(parts)

    def tile(t, carry):
        phi = acc[pl.ds(t, 1), :]
        tab[t, 7:8, :] = phi
        for n, part in enumerate(split3(phi)):
            parts[t, n : n + 1, :] = part
        return carry

    lax.fori_loop(0, TILES, tile, 0, unroll=8)
    for n in range(8):
        block = parts[16 * n : 16 * n + 16].reshape(128, 128)
        tall_phi[n] = jnp.transpose(block).astype(bf16)
    fill(sel, Y)
    probe = probe_bits()

    def spread(k, a, b, rows):
        rows[:, 0:384] = pair_values(tall, a, ghosts, b - TILES, sel)
        rows[:, 384:] = spread_phi(tall_phi, sel_phi, a)

    def use(k, a, b, rows):
        bb = b - TILES
        down = [None] * 3
        for w in range(16):
            y, sinv = unit(rows, w)
            keep = jnp.where(bit_mask(bits, k, w, probe), sinv * piece(rows, w, 3), 0.0)
            v = [keep * y[c] for c in range(3)]
            down = [q if d is None else d + q for d, q in zip(down, v)]
        for c in range(3):
            terms[bb, c : c + 1, :] += fold(down[c])

    over_slots(meta, GHOST_AT, meta[COUNT_AT + 1], None, spread, use, bufs)
    for n, cell in enumerate(cycle_cells):
        r, c = row_of(cell)
        if c == 0:
            out, at = to_left, r * GHOST
        elif c == 3:
            out, at = to_right, r * GHOST
        else:
            out, at = middle, (2 * (r // 3) + c - 1) * GHOST
        out[at : at + GHOST] = terms[n * GHOST : (n + 1) * GHOST]
    for t, out in ((0, to_left), (1, to_right)):
        for s in range(2):
            for g in range(GHOST):
                phi = acc[pl.ds(lists[s, t, g], 1), :]
                out[s * GHOST + g, 6:7, :] = phi
                middle[(2 * s + t) * GHOST + g, 6:7, :] = phi


def relay_kernel(from_left, from_right, middle, after, to_low, to_high):
    thick = (from_left, from_right)
    for s, out in ((0, to_low), (1, to_high)):
        for t in range(2):
            for g in range(GHOST):
                n, at = t * GHOST + g, (2 * s + t) * GHOST + g
                far = thick[t][3 * s * GHOST + g]
                out[n, 0:6, :] = middle[at, 0:6, :] + far[0:6, :]
                out[n, 6:7, :] = middle[at, 6:7, :]
                out[n, 7:8, :] = thick[t][s * GHOST + g, 6:7, :]


def local_force_kernel(half, meta, tab, tall, wide, tall_phi, sel_phi, bits, *refs):
    if half == 0:
        acc, sel, bufs = refs
        acc[...] = jnp.zeros_like(acc)
    else:
        unused, acc, sel, bufs = refs
    fill(sel, XY + (STIFF,))
    probe = probe_bits()

    def spread(k, a, b, rows):
        rows[:, 0:896] = pair_values(tall, a, wide, b, sel)
        rows[:, 896:] = spread_phi(tall_phi, sel_phi, a)

    def use(k, a, b, rows):
        phi = bcast_row(tab[b, 7:8, :])
        down = [None] * 3
        across = []
        for w in range(16):
            y, r2, s2, rinv, sinv = bond(rows, w)
            g = (s2 * sinv * rinv - 1.0) * piece(rows, w, 6) + (phi + piece(rows, w, 7))
            keep = jnp.where(bit_mask(bits, k, w, probe), sinv * g, 0.0)
            v = [keep * y[c] for c in range(3)]
            down = [q if d is None else d + q for d, q in zip(down, v)]
            across.append(merge3([lane_sum(q) for q in v]))
        sums = jnp.transpose(jnp.concatenate(across, 0))
        acc[a, 0:3, :] += sums[0:3, :]
        for c in range(3):
            acc[b, c : c + 1, :] -= fold(down[c])

    over_slots(meta, 0, meta[COUNT_AT], half, spread, use, bufs)


def force_kernel(
    meta, lists, tab, tall, tall_phi, sel_phi, ghosts, bits, local, rows_in, from_left, from_right,
    from_low, from_high, force, acc, back, sel, gphi, bufs,
):
    for n, cell in enumerate(cycle_cells):
        r, c = row_of(cell)
        if r in (0, 3):
            src, at, line = (from_low if r == 0 else from_high), (c // 2) * GHOST, (7, 6, 6, 7)[c]
        else:
            src, at, line = (from_left if c == 0 else from_right), (r - 1) * GHOST, 6
        for g in range(GHOST):
            gphi[n * GHOST + g : n * GHOST + g + 1, :] = src[at + g, line : line + 1, :]

    acc[...] = local[...] + rows_in[...]
    fill(sel, Y)
    probe = probe_bits()

    def spread(k, a, b, rows):
        rows[:, 0:384] = pair_values(tall, a, ghosts, b - TILES, sel)
        rows[:, 384:] = spread_phi(tall_phi, sel_phi, a)

    def use(k, a, b, rows):
        bb = b - TILES
        phi = bcast_row(gphi[pl.ds(bb, 1), :])
        across = []
        for w in range(16):
            y, sinv = unit(rows, w)
            both = phi + piece(rows, w, 3)
            keep = jnp.where(bit_mask(bits, k, w, probe), sinv * both, 0.0)
            across.append(merge3([lane_sum(keep * y[c]) for c in range(3)]))
        sums = jnp.transpose(jnp.concatenate(across, 0))
        acc[a, 0:3, :] += sums[0:3, :]

    over_slots(meta, GHOST_AT, meta[COUNT_AT + 1], None, spread, use, bufs)
    for n, q, g, s, t in listed(lists):
        thick = (from_left, from_right)[t][(1 + s) * GHOST + g]
        both = thick + (from_low, from_high)[s][t * GHOST + g]
        back[n, 0:3, :] = both[0:3, :] + tab[q, 7:8, :] * both[3:6, :]
    for n, q, g, s, t in listed(lists):
        acc[q, 0:3, :] -= back[n, 0:3, :]

    def store(t, carry):
        force[:, pl.ds(pl.multiple_of(t * 128, 128), 128)] = acc[t, 0:3, :]
        return carry

    lax.fori_loop(0, TILES, store, 0, unroll=8)


def swap(to_low, to_high, axis):
    count = lax.axis_size(axis)
    even = lax.axis_index(axis) % 2 == 0
    first = [(i, i ^ 1) for i in range(count)]
    second = [(i, i + 1 if i % 2 else i - 1) for i in range(1, count - 1)]
    one = lax.ppermute(jnp.where(even, to_high, to_low), axis, first)
    two = lax.ppermute(jnp.where(even, to_low, to_high), axis, second)
    return jnp.where(even, two, one), jnp.where(even, one, two)


def body(
    ref_pos, displacement, weighted_volume, corner_lists, row_tiles, column_tiles, bond_count,
    masks, broken,
):
    m = weighted_volume.reshape(TILES, 128)
    table, low, high, meta, lists = call(
        pack_kernel,
        "pack",
        (
            shape(TILES, 8, 128),
            shape(2 * GHOST, 8, 128),
            shape(2 * GHOST, 8, 128),
            shape(META, dtype=i32),
            shape(2, 2, GHOST, dtype=i32),
        ),
        [HBM] * 7,
        [VM, VM, VM, SM, SM],
        scratch=[
            pltpu.VMEM((3, TILES * 128), f32),
            pltpu.VMEM((3, TILES * 128), f32),
            pltpu.VMEM((TILES, 128), f32),
            pltpu.SMEM((SLOTS,), i32),
            pltpu.SMEM((SLOTS,), i32),
            pltpu.SMEM((1,), i32),
            pltpu.SemaphoreType.DMA((7,)),
        ],
        grant=PACK_GRANT,
    )(ref_pos, displacement, m, corner_lists, row_tiles, column_tiles, bond_count)

    def sel(n):
        return pltpu.VMEM((2 * PARTS, 128 * n), bf16)

    def bufs(n):
        return pltpu.VMEM((2, GROUP, 128, 128 * n), f32)

    from_low, from_high = swap(low, high, "slab")
    masks, broken, meta = lax.optimization_barrier((masks, broken, meta))
    intact = jnp.pad(masks & ~broken, ((0, 1), (0, 0), (0, 0)))
    bits, acc, tall, wide, sel_phi = call(
        functools.partial(local_stretch_kernel, 0),
        "stretch_a",
        (
            shape(SLOTS + 1, 16, 128, dtype=i32),
            shape(TILES, 128),
            shape(TILES, 128, 2 * PARTS, dtype=bf16),
            shape(TILES, PARTS, 128, dtype=bf16),
            shape(16, 128, 128, dtype=bf16),
        ),
        [SM, VM, VM],
        aliases={2: 0},
        scratch=[sel(6), bufs(6)],
        flops=1 << 26,
    )(meta, table, intact)
    side = call(
        side_kernel,
        "side",
        (shape(4 * GHOST, 8, 128), shape(4 * GHOST, 8, 128)),
        [VM] * 4 + [ANY],
    )(from_low, low, high, from_high, acc)
    left, right = swap(side[0], side[1], "thick")
    (acc,) = call(
        functools.partial(local_stretch_kernel, 1),
        "stretch_b",
        (shape(TILES, 128),),
        [SM] + [VM] * 4,
        aliases={4: 0},
        scratch=[sel(6), bufs(6)],
        flops=1 << 26,
    )(meta, bits, tall, wide, acc)

    acc, ghosts, to_left, to_right, middle = call(
        ghost_stretch_kernel,
        "ghost_stretch",
        (
            shape(TILES, 128),
            shape(CELLS * GHOST, PARTS, 128, dtype=bf16),
            shape(4, GHOST, 128),
            shape(4, GHOST, 128),
            shape(4, GHOST, 128),
        ),
        [SM] + [VM] * 7,
        aliases={7: 0},
        scratch=[pltpu.VMEM((CELLS * GHOST, 128), f32), sel(6), bufs(6)],
    )(meta, tall, bits, from_low, from_high, left, right, acc)

    back_left, back_right = swap(to_left, to_right, "thick")
    terms = call(
        functools.partial(ghost_terms_kernel, 0),
        "ghost_terms_a",
        (shape(TILES, 8, 128), shape(CELLS * GHOST, 8, 128)),
        [SM, VM, VM, VM],
        scratch=[sel(7), bufs(7)],
        flops=1 << 26,
    )(meta, tall, ghosts, bits)
    to_low, to_high = call(
        middle_kernel,
        "middle",
        (shape(2, GHOST, 128), shape(2, GHOST, 128)),
        [VM] * 3 + [ANY],
    )(middle, back_left, back_right, terms[0])
    back_low, back_high = swap(to_low, to_high, "slab")
    row_terms, column_terms = call(
        functools.partial(ghost_terms_kernel, 1),
        "ghost_terms_b",
        (shape(TILES, 8, 128), shape(CELLS * GHOST, 8, 128)),
        [SM] + [VM] * 5,
        aliases={4: 0, 5: 1},
        scratch=[sel(7), bufs(7)],
        flops=1 << 26,
    )(meta, tall, ghosts, bits, *terms)

    unused, table, tall_phi, dilatation, to_left, to_right, middle = call(
        dilatation_kernel,
        "dilatation",
        (
            shape(CELLS * GHOST, 8, 128),
            shape(TILES, 8, 128),
            shape(8, 128, 128, dtype=bf16),
            shape(TILES, 128),
            shape(4 * GHOST, 8, 128),
            shape(4 * GHOST, 8, 128),
            shape(4 * GHOST, 8, 128),
        ),
        [SM, SM] + [VM] * 12,
        aliases={13: 0, 2: 1},
        scratch=[
            pltpu.VMEM((TILES, 128), f32),
            pltpu.VMEM((TILES, 8, 128), f32),
            pltpu.VMEM((LISTS, 128), f32),
            sel(3),
            bufs(4),
        ],
    )(
        meta, lists, table, tall, sel_phi, ghosts, bits, acc, m, back_left, back_right, back_low,
        back_high, column_terms,
    )

    from_left, from_right = swap(to_left, to_right, "thick")
    (local,) = call(
        functools.partial(local_force_kernel, 0),
        "force_a",
        (shape(TILES, 8, 128),),
        [SM] + [VM] * 6,
        scratch=[sel(7), bufs(8)],
        flops=1 << 26,
    )(meta, table, tall, wide, tall_phi, sel_phi, bits)
    to_low, to_high = call(
        relay_kernel,
        "relay",
        (shape(2 * GHOST, 8, 128), shape(2 * GHOST, 8, 128)),
        [VM] * 3 + [ANY],
    )(from_left, from_right, middle, local)
    from_low, from_high = swap(to_low, to_high, "slab")
    (local,) = call(
        functools.partial(local_force_kernel, 1),
        "force_b",
        (shape(TILES, 8, 128),),
        [SM] + [VM] * 7,
        aliases={7: 0},
        scratch=[sel(7), bufs(8)],
        flops=1 << 26,
    )(meta, table, tall, wide, tall_phi, sel_phi, bits, local)
    (force,) = call(
        force_kernel,
        "force",
        (shape(3, TILES * 128),),
        [SM, SM] + [VM] * 12,
        scratch=[
            pltpu.VMEM((TILES, 8, 128), f32),
            pltpu.VMEM((LISTS, 8, 128), f32),
            sel(3),
            pltpu.VMEM((CELLS * GHOST, 128), f32),
            bufs(4),
        ],
    )(
        meta, lists, table, tall, tall_phi, sel_phi, ghosts, bits, local, row_terms, from_left,
        from_right, from_low, from_high,
    )
    return force, dilatation.reshape(TILES * 128)


def solution(mesh):
    in_specs = (
        P(None, ("slab", "thick")),
        P(None, ("slab", "thick")),
        P(("slab", "thick")),
        P(None, None, ("slab", "thick")),
        P(("slab", "thick")),
        P(("slab", "thick")),
        P(("slab", "thick")),
        P(("slab", "thick"), None, None),
        P(("slab", "thick"), None, None),
    )
    out_specs = (P(None, ("slab", "thick")), P(("slab", "thick")))
    return jax.shard_map(body, mesh=mesh, in_specs=in_specs, out_specs=out_specs, check_vma=False)
```

```python
import functools

import jax
import jax.numpy as jnp
from jax import lax
from jax.experimental import pallas as pl
from jax.experimental.pallas import tpu as pltpu
from jax.sharding import PartitionSpec as P

young = 25.0
poisson = 0.22
bulk_modulus = young / (3.0 * (1.0 - 2.0 * poisson))
shear_modulus = young / (2.0 * (1.0 + poisson))
volumetric_term = 3.0 * bulk_modulus - 5.0 * shear_modulus
shear_term = 15.0 * shear_modulus
radius_floor = 0.5
floor_squared = radius_floor * radius_floor

TILES = 128
SLOTS = 128
GHOST = 16
CELLS = 12
LISTS = 4 * GHOST
GROUP = 4
DUMMIES = 3 * GROUP
GHOST_AT = 144
COUNT_AT = 288
META = 296

PACK_GRANT = 67043328 - (900 << 10)

f32 = jnp.float32
bf16 = jnp.bfloat16
PARTS = 32
i32 = jnp.int32
VM = pl.BlockSpec(memory_space=pltpu.VMEM)
SM = pl.BlockSpec(memory_space=pltpu.SMEM)
ANY = pl.BlockSpec(memory_space=pl.ANY)
HBM = pl.BlockSpec(memory_space=pltpu.HBM)


def shape(*dims, dtype=f32):
    return jax.ShapeDtypeStruct(dims, dtype)


def call(
    kernel, name, outs, ins, out_spaces=None, aliases=None, scratch=(), flops=0, grant=24 << 20
):
    def run(*args):
        return pl.pallas_call(
            kernel,
            out_shape=outs,
            in_specs=list(ins),
            out_specs=list(out_spaces or [VM] * len(outs)),
            scratch_shapes=list(scratch),
            input_output_aliases=aliases or {},
            compiler_params=pltpu.CompilerParams(
                vmem_limit_bytes=grant,
            ),
            cost_estimate=pl.CostEstimate(flops=flops, bytes_accessed=1 << 20, transcendentals=0),
            name=name,
        )(*args)

    return run


def bcast_row(row):
    return jnp.broadcast_to(row, (8, 128))


def lane(column):
    return jnp.broadcast_to(column, (8, 128))


def fold(block):
    return jnp.sum(block, axis=0, keepdims=True)


def listed(lists):
    for s in range(2):
        for t in range(2):
            for g in range(GHOST):
                yield (2 * s + t) * GHOST + g, lists[s, t, g], g, s, t


def decode(code):
    return code & 255, (code >> 8) & 255, code >> 16


def over_slots(meta, base, count, half, spread, use, bufs):
    total = lax.div(count + (2 * GROUP - 1), 2 * GROUP)
    mid = lax.div(total + 1, 2)
    lo, hi = {None: (0, total), 0: (0, mid), 1: (mid, total)}[half]

    def ahead(group, buf):
        for i in range(GROUP):
            spread(*decode(meta[base + group * GROUP + i]), buf.at[i])

    def work(group, buf):
        for i in range(GROUP):
            use(*decode(meta[base + group * GROUP + i]), buf.at[i])

    ahead(2 * lo, bufs.at[0])

    def step(i, carry):
        ahead(2 * i + 1, bufs.at[1])
        work(2 * i, bufs.at[0])
        ahead(2 * i + 2, bufs.at[0])
        work(2 * i + 1, bufs.at[1])
        return carry

    lax.fori_loop(lo, hi, step, 0)


def bit_mask(bits, k, w, probe):
    return (bcast_row(bits[k, w : w + 1, :]) & probe) != 0


def probe_bits():
    return jnp.left_shift(jnp.int32(1), lax.broadcasted_iota(i32, (8, 128), 0))


def pack_kernel(
    x_in, u_in, m_in, lists_in, rows_in, cols_in, count_in, table, low, high, first, second,
    meta, lists, x, u, m,
    rows, cols, count, sems,
):
    pairs = (
        (x_in, x), (u_in, u), (m_in, m), (lists_in, lists), (rows_in, rows), (cols_in, cols),
        (count_in, count),
    )
    copies = [pltpu.make_async_copy(a, b, sems.at[n]) for n, (a, b) in enumerate(pairs)]
    for copy in copies:
        copy.start()
    for copy in copies:
        copy.wait()
    m[...] = shear_term / m[...]
    zero = jnp.zeros((1, 128), f32)

    def tile(t, carry):
        at = pl.ds(pl.multiple_of(t * 128, 128), 128)
        table[t, 0:3, :] = x[:, at]
        table[t, 3:6, :] = u[:, at]
        table[t, 6:7, :] = m[pl.ds(t, 1), :]
        table[t, 7:8, :] = zero
        return carry

    lax.fori_loop(0, TILES, tile, 0, unroll=8)
    for side, out in ((0, low), (1, high)):
        for g in range(2 * GHOST):
            out[g] = table[lists[side, g // GHOST, g % GHOST]]
    up = 1 - lax.axis_index("slab") % 2
    for side, out in ((up, first), (1 - up, second)):
        for g in range(2 * GHOST):
            out[g] = table[lists[side, g // GHOST, g % GHOST]]

    def sort(k, carry):
        nl, ng = carry
        b = cols[k]
        code = k + rows[k] * 256 + b * 65536
        ghost = (b >= TILES).astype(i32)
        meta[nl] = code
        meta[GHOST_AT + ng] = code
        return nl + 1 - ghost, ng + ghost

    nl, ng = lax.fori_loop(0, count[0], sort, (jnp.int32(0), jnp.int32(0)))
    for n in range(DUMMIES):
        meta[nl + n] = SLOTS
        meta[GHOST_AT + ng + n] = SLOTS + TILES * 65536
    meta[COUNT_AT] = nl
    meta[COUNT_AT + 1] = ng


def split3(v):
    hi = v.astype(bf16).astype(f32)
    rest = v - hi
    mid = rest.astype(bf16).astype(f32)
    return hi, mid, rest - mid


def parts_of(block):
    return jnp.concatenate(list(split3(block)) + [jnp.zeros((8, 128), f32)], 0)


ALL = tuple((c,) for c in range(3)) + tuple((c, 3 + c) for c in range(3)) + ((6,),)
XY = (0, 6)
XYS = (0, 7)
Y = (3, 6)


def selector(blocks, own):
    wide = 128 * len(blocks)
    row = lax.broadcasted_iota(i32, (PARTS, wide), 0)
    c = row & 7
    n = lax.broadcasted_iota(i32, (PARTS, wide), 1) >> 7
    out = jnp.zeros((PARTS, wide), f32)
    for at, names in enumerate(blocks):
        for name in names:
            value = -1.0 if own and name != 6 else 1.0
            out = jnp.where((n == at) & (c == name) & (row < 24), value, out)
    return out.astype(bf16)


def pair_values(tall, a, other, b, sel, blocks):
    theirs = other[b]
    at = slice(128 * blocks[0], 128 * blocks[1])
    right = jnp.concatenate([theirs] * (blocks[1] - blocks[0]), 1) * sel[PARTS:, at]
    return jnp.dot(
        tall[a], jnp.concatenate([sel[0:PARTS, at], right], 0), preferred_element_type=f32
    )


def fill(sel, blocks):
    sel[0:PARTS, :] = selector(blocks, True)
    sel[PARTS:, :] = selector(blocks, False)


def spread_phi(tall_phi, sel_phi, a):
    return jnp.dot(tall_phi[a >> 4], sel_phi[a & 15], preferred_element_type=f32)


def piece(rows, w, c):
    return rows[8 * w : 8 * w + 8, 128 * c : 128 * c + 128]


def length2(v):
    return jnp.maximum(v[0] * v[0] + v[1] * v[1] + v[2] * v[2], floor_squared)


def bond(rows, w):
    r2 = length2([piece(rows, w, c) for c in range(3)])
    y = [piece(rows, w, 3 + c) for c in range(3)]
    s2 = length2(y)
    return y, r2, s2, lax.rsqrt(r2), lax.rsqrt(s2)


def unit(rows, w):
    y = [piece(rows, w, c) for c in range(3)]
    return y, lax.rsqrt(length2(y))


def lane_sum(block):
    return jnp.sum(block, axis=1, keepdims=True)


def merge3(parts):
    lan = lax.broadcasted_iota(i32, (8, 128), 1)
    return jnp.where(lan == 0, lane(parts[0]), jnp.where(lan == 1, lane(parts[1]), lane(parts[2])))


def stretch_slot(tall, sel, other, base, bits, probe, row_acc, col_acc):
    def spread(k, a, b, rows):
        rows[...] = pair_values(tall, a, other, b - base, sel, XY)

    def use(k, a, b, rows):
        bb = b - base
        down = None
        across = []
        for w in range(16):
            y, r2, s2, rinv, sinv = bond(rows, w)
            e = s2 * sinv - r2 * rinv
            e = jnp.where(bit_mask(bits, k, w, probe), e, 0.0)
            down = e if down is None else down + e
            across.append(lane(lane_sum(e)))
        sums = jnp.transpose(jnp.concatenate(across, 0))[0:1, :]
        row_acc[pl.ds(a, 1), :] += sums
        col_acc[pl.ds(bb, 1), :] += fold(down)

    return spread, use


def local_stretch_kernel(half, meta, *refs):
    if half == 0:
        tab, unused, bits, acc, tall, wide, sel_phi, sel, bufs = refs
        fill(sel, ALL)
        acc[...] = jnp.zeros_like(acc)
        ones = jnp.ones((PARTS, 128), bf16)

        def stand(t, carry):
            parts = parts_of(tab[t]).astype(bf16)
            wide[t] = parts
            tall[t] = jnp.transpose(jnp.concatenate([parts, ones], 0))
            return carry

        lax.fori_loop(0, TILES, stand, 0, unroll=8)
        k = lax.broadcasted_iota(i32, (128, 128), 0)
        for n in range(16):
            sel_phi[n] = jnp.where(((k >> 3) == n) & ((k & 7) < 3), 1.0, 0.0).astype(bf16)
        w = lax.broadcasted_iota(i32, (16, 128), 0)
        j = lax.broadcasted_iota(i32, (16, 128), 1)
        below = jnp.zeros((16, 128), i32)
        for b in range(8):
            below += jnp.where(8 * w + b < j, 1 << b, 0)

        def own(i, carry):
            k, a, b = decode(meta[i])

            @pl.when(a == b)
            def _():
                bits[k] = bits[k] & below

            return carry

        lax.fori_loop(0, meta[COUNT_AT], own, 0)
    else:
        bits, tall, wide, sel, unused, acc, bufs = refs
    over_slots(
        meta,
        0,
        meta[COUNT_AT],
        half,
        *stretch_slot(tall, sel, wide, 0, bits, probe_bits(), acc, acc),
        bufs,
    )


def side_kernel(from_low, low, high, from_high, after, to_left, to_right):
    for n, part in enumerate((from_low, low, high, from_high)):
        to_left[n * GHOST : (n + 1) * GHOST] = part[0:GHOST]
        to_right[n * GHOST : (n + 1) * GHOST] = part[GHOST:]


def row_of(cell):
    return cell // 4, cell % 4


cycle_cells = (0, 1, 2, 3, 4, 7, 8, 11, 12, 13, 14, 15)


def ghost_stretch_kernel(
    meta, tall, bits, low, high, left, right, sel, unused, acc, ghosts, to_left, to_right, middle,
    gacc, bufs,
):
    for n, cell in enumerate(cycle_cells):
        r, c = row_of(cell)
        if c == 0:
            src, at = left, r * GHOST
        elif c == 3:
            src, at = right, r * GHOST
        else:
            src, at = (low if r == 0 else high), (c - 1) * GHOST
        for g in range(GHOST):
            ghosts[n * GHOST + g] = parts_of(src[at + g]).astype(bf16)
    gacc[...] = jnp.zeros_like(gacc)
    probe = probe_bits()
    over_slots(
        meta,
        GHOST_AT,
        meta[COUNT_AT + 1],
        None,
        *stretch_slot(tall, sel, ghosts, TILES, bits, probe, acc, gacc),
        bufs,
    )
    for n, cell in enumerate(cycle_cells):
        r, c = row_of(cell)
        part = gacc[n * GHOST : (n + 1) * GHOST, :]
        if c == 0:
            to_left[r] = part
        elif c == 3:
            to_right[r] = part
        else:
            middle[2 * (r // 3) + c - 1] = part


def middle_kernel(middle, left, right, after, to_low, to_high):
    for t, thick in ((0, left), (1, right)):
        to_low[t] = middle[t] + thick[0]
        to_high[t] = middle[2 + t] + thick[3]


def ghost_terms_kernel(half, meta, tall, ghosts, bits, sel, *refs):
    if half == 0:
        rows_out, cols_out, bufs = refs
        rows_out[...] = jnp.zeros_like(rows_out)
        cols_out[...] = jnp.zeros_like(cols_out)
    else:
        unused0, unused1, rows_out, cols_out, bufs = refs
    probe = probe_bits()

    def spread(k, a, b, rows):
        rows[...] = pair_values(tall, a, ghosts, b - TILES, sel, XYS)

    def use(k, a, b, rows):
        bb = b - TILES
        down = [None] * 6
        across = []
        for w in range(16):
            y, r2, s2, rinv, sinv = bond(rows, w)
            g = (s2 * sinv * rinv - 1.0) * piece(rows, w, 6)
            keep = jnp.where(bit_mask(bits, k, w, probe), sinv, 0.0)
            v = [keep * y[c] for c in range(3)]
            p = [g * v[c] for c in range(3)]
            down = [q if d is None else d + q for d, q in zip(down, p + v)]
            across.append(merge3([lane_sum(q) for q in p]))
        sums = jnp.transpose(jnp.concatenate(across, 0))
        rows_out[a, 0:3, :] += sums[0:3, :]
        for c in range(6):
            cols_out[bb, c : c + 1, :] += fold(down[c])

    over_slots(meta, GHOST_AT, meta[COUNT_AT + 1], half, spread, use, bufs)


def dilatation_kernel(
    meta, lists, tab_in, tall, sel_phi, ghosts, bits, acc_in, m, from_left, from_right, from_low,
    from_high, sel, terms_in, terms, tab, tall_phi, dil, to_left, to_right, middle, acc, parts, back,
    bufs,
):
    acc[...] = acc_in[...]
    for s in range(2):
        for t in range(2):
            at = (2 * s + t) * GHOST
            back[at : at + GHOST, :] = (
                (from_left, from_right)[t][1 + s] + (from_low, from_high)[s][t]
            )
    for n, q, g, s, t in listed(lists):
        acc[pl.ds(q, 1), :] += back[n : n + 1, :]
    theta = 3.0 * acc[...] / m[...]
    dil[...] = theta
    acc[...] = volumetric_term * theta / m[...]

    parts[...] = jnp.zeros_like(parts)

    def tile(t, carry):
        phi = acc[pl.ds(t, 1), :]
        tab[t, 7:8, :] = phi
        for n, part in enumerate(split3(phi)):
            parts[t, n : n + 1, :] = part
        return carry

    lax.fori_loop(0, TILES, tile, 0, unroll=8)
    for n in range(8):
        block = parts[16 * n : 16 * n + 16].reshape(128, 128)
        tall_phi[n] = jnp.transpose(block).astype(bf16)
    probe = probe_bits()

    def spread(k, a, b, rows):
        rows[:, 0:384] = pair_values(tall, a, ghosts, b - TILES, sel, Y)
        rows[:, 384:] = spread_phi(tall_phi, sel_phi, a)

    def use(k, a, b, rows):
        bb = b - TILES
        down = [None] * 3
        for w in range(16):
            y, sinv = unit(rows, w)
            keep = jnp.where(bit_mask(bits, k, w, probe), sinv * piece(rows, w, 3), 0.0)
            v = [keep * y[c] for c in range(3)]
            down = [q if d is None else d + q for d, q in zip(down, v)]
        for c in range(3):
            terms[bb, c : c + 1, :] += fold(down[c])

    over_slots(meta, GHOST_AT, meta[COUNT_AT + 1], None, spread, use, bufs)
    for n, cell in enumerate(cycle_cells):
        r, c = row_of(cell)
        if c == 0:
            out, at = to_left, r * GHOST
        elif c == 3:
            out, at = to_right, r * GHOST
        else:
            out, at = middle, (2 * (r // 3) + c - 1) * GHOST
        out[at : at + GHOST] = terms[n * GHOST : (n + 1) * GHOST]
    for t, out in ((0, to_left), (1, to_right)):
        for s in range(2):
            for g in range(GHOST):
                phi = acc[pl.ds(lists[s, t, g], 1), :]
                out[s * GHOST + g, 6:7, :] = phi
                middle[(2 * s + t) * GHOST + g, 6:7, :] = phi


def relay_kernel(from_left, from_right, middle, after, to_low, to_high):
    thick = (from_left, from_right)
    for s, out in ((0, to_low), (1, to_high)):
        for t in range(2):
            for g in range(GHOST):
                n, at = t * GHOST + g, (2 * s + t) * GHOST + g
                far = thick[t][3 * s * GHOST + g]
                out[n, 0:6, :] = middle[at, 0:6, :] + far[0:6, :]
                out[n, 6:7, :] = middle[at, 6:7, :]
                out[n, 7:8, :] = thick[t][s * GHOST + g, 6:7, :]


def local_force_kernel(half, meta, tab, tall, wide, tall_phi, sel_phi, bits, sel, *refs):
    if half == 0:
        acc, bufs = refs
        acc[...] = jnp.zeros_like(acc)
    else:
        unused, acc, bufs = refs
    probe = probe_bits()

    def spread(k, a, b, rows):
        rows[:, 0:896] = pair_values(tall, a, wide, b, sel, XYS)
        rows[:, 896:] = spread_phi(tall_phi, sel_phi, a)

    def use(k, a, b, rows):
        phi = bcast_row(tab[b, 7:8, :])
        down = [None] * 3
        across = []
        for w in range(16):
            y, r2, s2, rinv, sinv = bond(rows, w)
            g = (s2 * sinv * rinv - 1.0) * piece(rows, w, 6) + (phi + piece(rows, w, 7))
            keep = jnp.where(bit_mask(bits, k, w, probe), sinv * g, 0.0)
            v = [keep * y[c] for c in range(3)]
            down = [q if d is None else d + q for d, q in zip(down, v)]
            across.append(merge3([lane_sum(q) for q in v]))
        sums = jnp.transpose(jnp.concatenate(across, 0))
        acc[a, 0:3, :] += sums[0:3, :]
        for c in range(3):
            acc[b, c : c + 1, :] -= fold(down[c])

    over_slots(meta, 0, meta[COUNT_AT], half, spread, use, bufs)


def force_kernel(
    meta, lists, tab, tall, tall_phi, sel_phi, ghosts, bits, local, rows_in, from_left, from_right,
    from_low, from_high, sel, force, acc, back, gphi, bufs,
):
    for n, cell in enumerate(cycle_cells):
        r, c = row_of(cell)
        if r in (0, 3):
            src, at, line = (from_low if r == 0 else from_high), (c // 2) * GHOST, (7, 6, 6, 7)[c]
        else:
            src, at, line = (from_left if c == 0 else from_right), (r - 1) * GHOST, 6
        for g in range(GHOST):
            gphi[n * GHOST + g : n * GHOST + g + 1, :] = src[at + g, line : line + 1, :]

    acc[...] = local[...] + rows_in[...]
    probe = probe_bits()

    def spread(k, a, b, rows):
        rows[:, 0:384] = pair_values(tall, a, ghosts, b - TILES, sel, Y)
        rows[:, 384:] = spread_phi(tall_phi, sel_phi, a)

    def use(k, a, b, rows):
        bb = b - TILES
        phi = bcast_row(gphi[pl.ds(bb, 1), :])
        across = []
        for w in range(16):
            y, sinv = unit(rows, w)
            both = phi + piece(rows, w, 3)
            keep = jnp.where(bit_mask(bits, k, w, probe), sinv * both, 0.0)
            across.append(merge3([lane_sum(keep * y[c]) for c in range(3)]))
        sums = jnp.transpose(jnp.concatenate(across, 0))
        acc[a, 0:3, :] += sums[0:3, :]

    over_slots(meta, GHOST_AT, meta[COUNT_AT + 1], None, spread, use, bufs)
    for n, q, g, s, t in listed(lists):
        thick = (from_left, from_right)[t][(1 + s) * GHOST + g]
        both = thick + (from_low, from_high)[s][t * GHOST + g]
        back[n, 0:3, :] = both[0:3, :] + tab[q, 7:8, :] * both[3:6, :]
    for n, q, g, s, t in listed(lists):
        acc[q, 0:3, :] -= back[n, 0:3, :]

    def store(t, carry):
        force[:, pl.ds(pl.multiple_of(t * 128, 128), 128)] = acc[t, 0:3, :]
        return carry

    lax.fori_loop(0, TILES, store, 0, unroll=8)


def swap(to_low, to_high, axis):
    even = lax.axis_index(axis) % 2 == 0
    return exchange(
        jnp.where(even, to_high, to_low), jnp.where(even, to_low, to_high), axis
    )


def exchange(sent_first, sent_second, axis):
    count = lax.axis_size(axis)
    even = lax.axis_index(axis) % 2 == 0
    first = [(i, i ^ 1) for i in range(count)]
    second = [(i, i + 1 if i % 2 else i - 1) for i in range(1, count - 1)]
    one = lax.ppermute(sent_first, axis, first)
    two = lax.ppermute(sent_second, axis, second)
    return jnp.where(even, two, one), jnp.where(even, one, two)


def body(
    ref_pos, displacement, weighted_volume, corner_lists, row_tiles, column_tiles, bond_count,
    masks, broken,
):
    m = weighted_volume.reshape(TILES, 128)
    table, low, high, first, second, meta, lists = call(
        pack_kernel,
        "pack",
        (
            shape(TILES, 8, 128),
            *[shape(2 * GHOST, 8, 128)] * 4,
            shape(META, dtype=i32),
            shape(2, 2, GHOST, dtype=i32),
        ),
        [HBM] * 7,
        [VM] * 5 + [SM, SM],
        scratch=[
            pltpu.VMEM((3, TILES * 128), f32),
            pltpu.VMEM((3, TILES * 128), f32),
            pltpu.VMEM((TILES, 128), f32),
            pltpu.SMEM((SLOTS,), i32),
            pltpu.SMEM((SLOTS,), i32),
            pltpu.SMEM((1,), i32),
            pltpu.SemaphoreType.DMA((7,)),
        ],
        grant=PACK_GRANT,
    )(ref_pos, displacement, m, corner_lists, row_tiles, column_tiles, bond_count)

    def bufs(n):
        return pltpu.VMEM((2, GROUP, 128, 128 * n), f32)

    from_low, from_high = exchange(first, second, "slab")
    masks, broken, meta = lax.optimization_barrier((masks, broken, meta))
    intact = jnp.pad(masks & ~broken, ((0, 1), (0, 0), (0, 0)))
    bits, acc, tall, wide, sel_phi, sel = call(
        functools.partial(local_stretch_kernel, 0),
        "stretch_a",
        (
            shape(SLOTS + 1, 16, 128, dtype=i32),
            shape(TILES, 128),
            shape(TILES, 128, 2 * PARTS, dtype=bf16),
            shape(TILES, PARTS, 128, dtype=bf16),
            shape(16, 128, 128, dtype=bf16),
            shape(2 * PARTS, 128 * len(ALL), dtype=bf16),
        ),
        [SM, VM, VM],
        aliases={2: 0},
        scratch=[bufs(6)],
        flops=1 << 26,
    )(meta, table, intact)
    side = call(
        side_kernel,
        "side",
        (shape(4 * GHOST, 8, 128), shape(4 * GHOST, 8, 128)),
        [VM] * 4 + [ANY],
    )(from_low, low, high, from_high, acc)
    left, right = swap(side[0], side[1], "thick")
    (acc,) = call(
        functools.partial(local_stretch_kernel, 1),
        "stretch_b",
        (shape(TILES, 128),),
        [SM] + [VM] * 5,
        aliases={5: 0},
        scratch=[bufs(6)],
        flops=1 << 26,
    )(meta, bits, tall, wide, sel, acc)

    acc, ghosts, to_left, to_right, middle = call(
        ghost_stretch_kernel,
        "ghost_stretch",
        (
            shape(TILES, 128),
            shape(CELLS * GHOST, PARTS, 128, dtype=bf16),
            shape(4, GHOST, 128),
            shape(4, GHOST, 128),
            shape(4, GHOST, 128),
        ),
        [SM] + [VM] * 8,
        aliases={8: 0},
        scratch=[pltpu.VMEM((CELLS * GHOST, 128), f32), bufs(6)],
    )(meta, tall, bits, from_low, from_high, left, right, sel, acc)

    back_left, back_right = swap(to_left, to_right, "thick")
    terms = call(
        functools.partial(ghost_terms_kernel, 0),
        "ghost_terms_a",
        (shape(TILES, 8, 128), shape(CELLS * GHOST, 8, 128)),
        [SM] + [VM] * 4,
        scratch=[bufs(7)],
        flops=1 << 26,
    )(meta, tall, ghosts, bits, sel)
    to_low, to_high = call(
        middle_kernel,
        "middle",
        (shape(2, GHOST, 128), shape(2, GHOST, 128)),
        [VM] * 3 + [ANY],
    )(middle, back_left, back_right, terms[0])
    back_low, back_high = swap(to_low, to_high, "slab")
    row_terms, column_terms = call(
        functools.partial(ghost_terms_kernel, 1),
        "ghost_terms_b",
        (shape(TILES, 8, 128), shape(CELLS * GHOST, 8, 128)),
        [SM] + [VM] * 6,
        aliases={5: 0, 6: 1},
        scratch=[bufs(7)],
        flops=1 << 26,
    )(meta, tall, ghosts, bits, sel, *terms)

    unused, table, tall_phi, dilatation, to_left, to_right, middle = call(
        dilatation_kernel,
        "dilatation",
        (
            shape(CELLS * GHOST, 8, 128),
            shape(TILES, 8, 128),
            shape(8, 128, 128, dtype=bf16),
            shape(TILES, 128),
            shape(4 * GHOST, 8, 128),
            shape(4 * GHOST, 8, 128),
            shape(4 * GHOST, 8, 128),
        ),
        [SM, SM] + [VM] * 13,
        aliases={14: 0, 2: 1},
        scratch=[
            pltpu.VMEM((TILES, 128), f32),
            pltpu.VMEM((TILES, 8, 128), f32),
            pltpu.VMEM((LISTS, 128), f32),
            bufs(4),
        ],
    )(
        meta, lists, table, tall, sel_phi, ghosts, bits, acc, m, back_left, back_right, back_low,
        back_high, sel, column_terms,
    )

    from_left, from_right = swap(to_left, to_right, "thick")
    (local,) = call(
        functools.partial(local_force_kernel, 0),
        "force_a",
        (shape(TILES, 8, 128),),
        [SM] + [VM] * 7,
        scratch=[bufs(8)],
        flops=1 << 26,
    )(meta, table, tall, wide, tall_phi, sel_phi, bits, sel)
    to_low, to_high = call(
        relay_kernel,
        "relay",
        (shape(2 * GHOST, 8, 128), shape(2 * GHOST, 8, 128)),
        [VM] * 3 + [ANY],
    )(from_left, from_right, middle, local)
    from_low, from_high = swap(to_low, to_high, "slab")
    (local,) = call(
        functools.partial(local_force_kernel, 1),
        "force_b",
        (shape(TILES, 8, 128),),
        [SM] + [VM] * 8,
        aliases={8: 0},
        scratch=[bufs(8)],
        flops=1 << 26,
    )(meta, table, tall, wide, tall_phi, sel_phi, bits, sel, local)
    (force,) = call(
        force_kernel,
        "force",
        (shape(3, TILES * 128),),
        [SM, SM] + [VM] * 13,
        scratch=[
            pltpu.VMEM((TILES, 8, 128), f32),
            pltpu.VMEM((LISTS, 8, 128), f32),
            pltpu.VMEM((CELLS * GHOST, 128), f32),
            bufs(4),
        ],
    )(
        meta, lists, table, tall, tall_phi, sel_phi, ghosts, bits, local, row_terms, from_left,
        from_right, from_low, from_high, sel,
    )
    return force, dilatation.reshape(TILES * 128)


def solution(mesh):
    in_specs = (
        P(None, ("slab", "thick")),
        P(None, ("slab", "thick")),
        P(("slab", "thick")),
        P(None, None, ("slab", "thick")),
        P(("slab", "thick")),
        P(("slab", "thick")),
        P(("slab", "thick")),
        P(("slab", "thick"), None, None),
        P(("slab", "thick"), None, None),
    )
    out_specs = (P(None, ("slab", "thick")), P(("slab", "thick")))
    return jax.shard_map(body, mesh=mesh, in_specs=in_specs, out_specs=out_specs, check_vma=False)
```
